512 devices in a mesh: lat: 32 (over z, core), lev: 16 (over x, y).
Axes of the slice: x: 4, y: 4, z: 16, core: 2. Of those that a mesh axis runs over, the one named last changes fastest.
Arguments:
- zonal_wind: float32 [64, 256, 2880], P('lev', 'lat'), may hold values from -1 to 1
- merid_wind: float32 [64, 256, 2880], P('lev', 'lat'), may hold values from -1 to 1
- thickness: float32 [64, 256, 2880], P('lev', 'lat'), may hold values from 0.6 to 1.8
- potential_temp: float32 [64, 256, 2880], P('lev', 'lat'), may hold values from 0.5 to 2
- cutoff: int32 [32], replicated, may hold values from 4 to 255, as said below
- sigma_weights: float32 [64], replicated, may hold values from 0.5 to 2
Outputs:
- remapped_wind: float32 [64, 256, 2880], P(None, 'lat', 'lev')
- remapped_temp: float32 [64, 256, 2880], P(None, 'lat', 'lev')
The draws below stay inside these ranges and needn't reach their ends.
Inputs may be any that keep to these rules, and one draw needn't show every extreme that they name: `cutoff`: cutoff wavenumber of each filtered row, southern rows in row order, then northern rows in row order.
All inputs are finite; a program needn't handle non-finite values.
Results may differ from the reference program's by a relative error of at most 0.0003.
Values sent between devices are 32-bit elements; how exact they have to be, the bound alone decides.
No kernel may reach another device: no remote copies, remote signals or barrier semaphores. Data moves between devices by JAX's collectives and lax.ppermute only.
A program may use at most 64 MiB of HBM per device.

```python
import math
import jax
import jax.numpy as jnp
from jax import lax

IM = 2880
KMAX = 256
NLAT = 256
NLEV = 64
POLAR = 16


def draw_cutoff(key, part):
    row_count = 2 * POLAR
    position = jnp.arange(row_count, dtype=jnp.int32)
    distance = jnp.minimum(position, row_count - 1 - position)
    spacing = (KMAX - 4) // POLAR
    jitter = jax.random.randint(key, (row_count,), 0, spacing, dtype=jnp.int32)
    return (4 + distance * spacing + jitter).astype(jnp.int32)


def block_scale(stream_key, dims, pieces, least, top_value):
    level = 1.0
    for dim, shards_of in pieces:
        draws = jax.random.uniform(jax.random.fold_in(jax.random.fold_in(stream_key, 6), dim), (shards_of,), jnp.float32, least / len(pieces), top_value / len(pieces))
        level = level * jnp.repeat(jnp.exp(draws), dims[dim] // shards_of).reshape((-1,) + (1,) * (len(dims) - 1 - dim))
    return level


def setup_inputs(seed: int = 0) -> dict:
    splits = jax.random.split(jax.random.key(seed), 7)
    return {
        "zonal_wind": jnp.clip(jax.random.uniform(splits[0], (NLEV, NLAT, IM), jnp.float32, -1.0, 1.0) * block_scale(splits[0], (NLEV, NLAT, IM), ((0, 16), (1, 32)), -0.4, 0.0), -1.0, 1.0),
        "merid_wind": jnp.clip(jax.random.uniform(splits[1], (NLEV, NLAT, IM), jnp.float32, -1.0, 1.0) * block_scale(splits[1], (NLEV, NLAT, IM), ((0, 16), (1, 32)), -0.4, 0.0), -1.0, 1.0),
        "thickness": jnp.clip(jnp.exp(math.log(1.8) - 1.0986122 * jax.random.uniform(splits[2], (NLEV, NLAT, IM), jnp.float32) ** block_scale(splits[2], (NLEV, NLAT, IM), ((0, 16), (1, 32)), -0.2, 0.2)), 0.6, 1.8),
        "potential_temp": jnp.clip(jnp.exp(math.log(2.0) - 1.3862944 * jax.random.uniform(splits[3], (NLEV, NLAT, IM), jnp.float32) ** block_scale(splits[3], (NLEV, NLAT, IM), ((0, 16), (1, 32)), -0.2, 0.2)), 0.5, 2.0),
        "cutoff": draw_cutoff(jax.random.fold_in(splits[6], 71), 0),
        "sigma_weights": jnp.clip(jnp.exp(jax.random.uniform(splits[5], (NLEV,), jnp.float32, math.log(0.5), math.log(2.0))), 0.5, 2.0),
    }


COURANT = 0.02
PRESSURE_COEF = 0.05


def flux_zonal(quantity, wind):
    face_wind = 0.5 * (wind + jnp.roll(wind, 1, axis=-1))
    face_flux = face_wind * 0.5 * (quantity + jnp.roll(quantity, 1, axis=-1))
    return jnp.roll(face_flux, -1, axis=-1) - face_flux


def flux_merid(padded_field, padded_wind):
    face_flux = 0.25 * (padded_wind[:, :-1] + padded_wind[:, 1:]) * (padded_field[:, :-1] + padded_field[:, 1:])
    return face_flux[:, 1:] - face_flux[:, :-1]


def advance(thickness, potential, zonal, merid_pad, thick_pad, temp_pad):
    heat = thickness * potential
    heat_pad = thick_pad * temp_pad
    new_thick = thickness - COURANT * (flux_zonal(thickness, zonal) + flux_merid(thick_pad, merid_pad))
    new_heat = heat - COURANT * (flux_zonal(heat, zonal) + flux_merid(heat_pad, merid_pad))
    return new_thick, new_heat / new_thick


def pressure_push(zonal, mid_pressure):
    return zonal - PRESSURE_COEF * (jnp.roll(mid_pressure, -1, axis=-1) - jnp.roll(mid_pressure, 1, axis=-1))


def ppm_edges(fields):
    halves = 0.5 * (fields[:, :-1] + fields[:, 1:])
    fourth = (7.0 / 12.0) * (fields[:, 1:-2] + fields[:, 2:-1]) - (1.0 / 12.0) * (fields[:, :-3] + fields[:, 3:])
    return jnp.concatenate([fields[:, :1], halves[:, :1], fourth, halves[:, -1:], fields[:, -1:]], axis=1)


def remap_columns(fields, thickness, weights):
    levels = thickness.shape[0]
    field_count = fields.shape[0]
    flat_thick = thickness.reshape(levels, -1)
    flat_fields = fields.reshape(field_count, levels, -1)
    top_edges = jnp.cumsum(flat_thick, axis=0) - flat_thick
    surface = jnp.sum(flat_thick, axis=0)
    sigma_edges = (jnp.cumsum(weights) / jnp.sum(weights))[:, None]
    targets = surface[None] * sigma_edges
    previous = jnp.concatenate([jnp.zeros_like(targets[:1]), targets[:-1]], axis=0)
    edge_values = ppm_edges(flat_fields)
    left_edge = edge_values[:, :-1]
    curvature = 6.0 * (flat_fields - 0.5 * (left_edge + edge_values[:, 1:]))
    linear = edge_values[:, 1:] - left_edge + curvature

    def mass_block(edge_block):
        fraction = jnp.clip((edge_block[:, None] - top_edges[None]) / flat_thick[None], 0.0, 1.0)
        collected = []
        for member in range(field_count):
            partial_value = fraction * (left_edge[member][None] + fraction * (0.5 * linear[member][None] - fraction * curvature[member][None] / 3.0))
            collected.append(jnp.sum(flat_thick[None] * partial_value, axis=1))
        return tuple(collected)

    grouped = targets.reshape(levels // 8, 8, -1)
    masses = lax.map(mass_block, grouped)
    results = []
    for mass in masses:
        mass_below = mass.reshape(levels, -1)
        mass_above = jnp.concatenate([jnp.zeros_like(mass_below[:1]), mass_below[:-1]], axis=0)
        results.append((mass_below - mass_above) / (targets - previous))
    return jnp.stack(results).reshape(fields.shape)


def pad_rows(field):
    return jnp.pad(field, ((0, 0), (1, 1), (0, 0)))


def reference(zonal_wind, merid_wind, thickness, potential_temp, cutoff, sigma_weights):
    wind_pair = jnp.stack([zonal_wind, merid_wind])
    wavenumber = jnp.arange(IM // 2 + 1, dtype=jnp.int32)

    def smooth(rows_block, limits):
        spectrum = jnp.fft.rfft(rows_block, axis=-1)
        kept_mask = wavenumber[None, :] <= limits[:, None]
        spectrum = jnp.where(kept_mask, spectrum, 0.0)
        return jnp.fft.irfft(spectrum, n=IM, axis=-1).astype(rows_block.dtype)

    southern = smooth(wind_pair[:, :, :POLAR], cutoff[:POLAR])
    northern = smooth(wind_pair[:, :, NLAT - POLAR:], cutoff[POLAR:])
    wind_pair = jnp.concatenate([southern, wind_pair[:, :, POLAR:NLAT - POLAR], northern], axis=2)
    zonal = wind_pair[0]
    merid = wind_pair[1]
    new_thick, new_temp = advance(thickness, potential_temp, zonal, pad_rows(merid), pad_rows(thickness), pad_rows(potential_temp))
    mid_pressure = jnp.cumsum(new_thick, axis=0) - 0.5 * new_thick
    new_zonal = pressure_push(zonal, mid_pressure)
    fields = jnp.stack([new_zonal, new_temp])

    def remap_row(row_index):
        return remap_columns(lax.dynamic_slice_in_dim(fields, row_index, 1, 2), lax.dynamic_slice_in_dim(new_thick, row_index, 1, 1), sigma_weights)

    rows_out = lax.map(remap_row, jnp.arange(NLAT, dtype=jnp.int32))
    result = jnp.moveaxis(rows_out[:, :, :, 0], 0, 2)
    return result[0], result[1]
```

```python
import functools
import math

import jax
import jax.numpy as jnp
import numpy as np
from jax import lax
from jax.experimental import pallas as pl
from jax.experimental.pallas import tpu as pltpu
from jax.sharding import PartitionSpec as P

F32 = jnp.float32
BF16 = jnp.bfloat16

LON = 2880
EXT = 2944
CHUNKS = EXT // 128
LEVELS = 64
ROWS = 8
LEV_DEV = 4
BANDS = 32
PEERS = 16
PIECE = LON // PEERS
TAIL = PIECE - 128
RADIX = 5
PART = LON // RADIX
POLAR = 16
COURANT = 0.02
PRESSURE_COEF = 0.05
VEC = 80


def mode_table():
    j = np.arange(64)
    orders = [[5 * j], [5 * j + 1, 5 * j + 4], [5 * j + 2, 5 * j + 3]]
    r = np.arange(PART)
    columns = []
    for order in orders:
        waves = np.concatenate(order)
        angle = 2.0 * np.pi * ((r[:, None] * waves[None, :]) % LON) / LON
        columns += [np.cos(angle), np.sin(angle)]
    table = np.concatenate(columns, axis=1)
    high = table.astype(np.float32).astype(jnp.bfloat16)
    low = (table - high.astype(np.float64)).astype(np.float32).astype(jnp.bfloat16)
    return high, low


def split(x):
    high = x.astype(BF16)
    low = (x - high.astype(F32)).astype(BF16)
    return high, low


def dot3(x, high_ref, low_ref, first, count, transposed):
    dims = (((1,), (1,)), ((), ())) if transposed else (((1,), (0,)), ((), ()))
    x_high, x_low = split(x)
    t_high = high_ref[:, first : first + count]
    t_low = low_ref[:, first : first + count]
    dot = functools.partial(lax.dot_general, dimension_numbers=dims, preferred_element_type=F32)
    return dot(x_high, t_high) + (dot(x_low, t_high) + dot(x_high, t_low))


def spin(x, shift):
    shift = shift % 128
    return x if shift == 0 else pltpu.roll(x, shift, axis=1)


def filter_rows(x_ref, high_ref, low_ref, limit):
    c1, c2 = math.cos(2 * math.pi / 5), math.cos(4 * math.pi / 5)
    s1, s2 = math.sin(2 * math.pi / 5), math.sin(4 * math.pi / 5)
    x = [x_ref[:, PART * q : PART * (q + 1)] for q in range(RADIX)]
    sum1, dif1 = x[1] + x[4], x[1] - x[4]
    sum2, dif2 = x[2] + x[3], x[2] - x[3]
    z0 = x[0] + sum1 + sum2
    z1 = jnp.concatenate([x[0] + c1 * sum1 + c2 * sum2, s1 * dif1 + s2 * dif2], axis=0)
    z2 = jnp.concatenate([x[0] + c2 * sum1 + c1 * sum2, s2 * dif1 - s1 * dif2], axis=0)
    lane = lax.broadcasted_iota(jnp.int32, (VEC, 128), 1)
    half = lane < 64
    slot = jnp.where(half, lane, lane - 64)
    sign = jnp.where(half, 1.0, -1.0).astype(F32)

    wave0 = 5 * slot
    weight0 = jnp.where(wave0 <= limit, jnp.where(wave0 == 0, 1.0 / LON, 2.0 / LON), 0.0)
    spec0 = dot3(z0, high_ref, low_ref, 0, 128, False) * weight0
    back0 = dot3(spec0, high_ref, low_ref, 0, 128, True)
    backs = []
    for z, first, low_wave, high_wave in ((z1, 128, 1, 4), (z2, 384, 2, 3)):
        wave = 5 * slot + jnp.where(half, low_wave, high_wave)
        weight = jnp.where(wave <= limit, 2.0 / LON, 0.0)
        flip = weight * sign
        y = dot3(z, high_ref, low_ref, first, 256, False)
        cc, cs = y[:VEC, :128], y[:VEC, 128:]
        sc, ss = y[VEC:, :128], y[VEC:, 128:]
        a = cc - sign * ss
        b = cs + sign * sc
        even = jnp.concatenate([a * weight, b * weight], axis=1)
        odd = jnp.concatenate([b * flip, -(a * flip)], axis=1)
        back = dot3(jnp.concatenate([even, odd], axis=0), high_ref, low_ref, first, 256, True)
        backs += [back[:VEC], back[VEC:]]
    e1, o1, e2, o2 = backs
    out = [back0 + e1 + e2]
    p, m = back0 + c1 * e1 + c2 * e2, s1 * o1 + s2 * o2
    r, n = back0 + c2 * e1 + c1 * e2, s2 * o1 - s1 * o2
    return out + [p + m, r + n, r - n, p - m]


def dynamics_kernel(
    band_ref, cutoff_ref, u_ref, v_ref, h_ref, t_ref, south_ref, north_ref, high_ref, low_ref,
    out_ref, x_ref, y_ref, e_ref, halo_ref, n_ref,
):
    band = band_ref[0]
    lane = lax.broadcasted_iota(jnp.int32, (8, 128), 1)
    row = lax.broadcasted_iota(jnp.int32, (8, 128), 0)
    south_row = band * ROWS - 1
    north_row = band * ROWS + ROWS
    total_rows = BANDS * ROWS

    def is_polar(r):
        return jnp.logical_and(
            jnp.logical_and(r >= 0, r < total_rows),
            jnp.logical_or(r < POLAR, r >= total_rows - POLAR),
        )

    def entry(r):
        index = jnp.where(r < POLAR, r, r - (total_rows - 2 * POLAR))
        return cutoff_ref[jnp.clip(index, 0, 2 * POLAR - 1)]

    own = is_polar(band * ROWS)
    south = is_polar(south_row)
    north = is_polar(north_row)

    for f, ref in enumerate((u_ref, v_ref, h_ref, t_ref)):
        e_ref[f, :, :, 0:LON] = ref[...]
    for f in range(3):
        halo_ref[f, 0:4, 0:LON] = south_ref[f]
        halo_ref[f, 4:8, 0:LON] = north_ref[f]

    @pl.when(jnp.logical_or(own, jnp.logical_or(south, north)))
    def _():
        x_ref[0:32, :] = u_ref[...].reshape(32, LON)
        x_ref[32:64, :] = v_ref[...].reshape(32, LON)
        x_ref[64:68, :] = south_ref[0]
        x_ref[68:72, :] = north_ref[0]
        x_ref[72:80, :] = jnp.zeros((8, LON), F32)
        own_limit = jnp.zeros((8, 128), jnp.int32)
        for r in range(ROWS):
            own_limit = jnp.where(row == r, entry(band * ROWS + r), own_limit)
        halo_limit = jnp.where(row < 4, entry(south_row), entry(north_row))
        limit = jnp.concatenate([own_limit] * 8 + [halo_limit] * 2, axis=0)
        pieces = filter_rows(x_ref, high_ref, low_ref, limit)
        for q in range(RADIX):
            y_ref[:, PART * q : PART * (q + 1)] = pieces[q]

        @pl.when(own)
        def _():
            e_ref[0, :, :, 0:LON] = y_ref[0:32, :].reshape(4, 8, LON)
            e_ref[1, :, :, 0:LON] = y_ref[32:64, :].reshape(4, 8, LON)

        @pl.when(south)
        def _():
            halo_ref[0, 0:4, 0:LON] = y_ref[64:68, :]

        @pl.when(north)
        def _():
            halo_ref[0, 4:8, 0:LON] = y_ref[68:72, :]

    def wrap(ref, index):
        last = ref[index + (slice(None), slice(EXT - 128, EXT))]
        first = ref[index + (slice(None), slice(0, 128))]
        ref[index + (slice(None), slice(EXT - 128, EXT))] = jnp.where(
            lane < 64, last, jnp.where(lane < 96, spin(first, 64), spin(last, 64))
        )

    for f in range(4):
        for l in range(LEV_DEV):
            wrap(e_ref, (f, l))
    for f in range(3):
        wrap(halo_ref, (f,))

    scale = COURANT * 0.25
    for l in range(LEV_DEV):

        def load(f, i):
            return e_ref[f, l, :, 128 * i : 128 * (i + 1)]

        def side(f, r, i):
            return jnp.broadcast_to(halo_ref[f, r : r + 1, 128 * i : 128 * (i + 1)], (8, 128))

        i = CHUNKS - 1
        u, h = load(0, i), load(2, i)
        q = h * load(3, i)
        before = tuple(spin(z, 1) for z in (u, h, q))
        flux = {}
        state = {}
        for i in range(CHUNKS + 1):
            if i < CHUNKS:
                u, v, h = load(0, i), load(1, i), load(2, i)
                q = h * load(3, i)
                now = tuple(spin(z, 1) for z in (u, h, q))
                ul, hl, ql = (jnp.where(lane == 0, b, n) for b, n in zip(before, now))
                before = now
                face = u + ul
                fh, fq = face * (h + hl), face * (q + ql)
                turned = (spin(fh, -1), spin(fq, -1))
                if i == 0:
                    first = turned
                vs, hs = side(0, l, i), side(1, l, i)
                qs = hs * side(2, l, i)
                vn, hn = side(0, 4 + l, i), side(1, 4 + l, i)
                qn = hn * side(2, 4 + l, i)
                vm, hm, qm = (
                    jnp.where(row == 0, s, pltpu.roll(z, 1, axis=0))
                    for s, z in ((vs, v), (hs, h), (qs, q))
                )
                vp, hp, qp = (
                    jnp.where(row == 7, s, pltpu.roll(z, 7, axis=0))
                    for s, z in ((vn, v), (hn, h), (qn, q))
                )
                wm, wp = v + vm, v + vp
                gh = wp * (h + hp) - wm * (h + hm) - fh
                gq = wp * (q + qp) - wm * (q + qm) - fq
                state[i] = (h, q, gh, gq)
                flux[i] = turned
            if i >= 1:
                k = i - 1
                nxt = flux[i] if i < CHUNKS else first
                h0, q0, gh0, gq0 = state.pop(k)
                mine = flux.pop(k)
                rh = jnp.where(lane == 127, nxt[0], mine[0])
                rq = jnp.where(lane == 127, nxt[1], mine[1])
                new_h = h0 - scale * (rh + gh0)
                new_q = q0 - scale * (rq + gq0)
                n_ref[0, l, :, 128 * k : 128 * (k + 1)] = new_h
                n_ref[1, l, :, 128 * k : 128 * (k + 1)] = new_q / new_h

    def fetch(f, l, i):
        if f == 0:
            return e_ref[0, l, :, 128 * i : 128 * (i + 1)]
        return n_ref[2 - f, l, :, 128 * i : 128 * (i + 1)]

    for j in range(PEERS):
        for f in range(3):
            for pair in range(2):
                tails = []
                for l in (2 * pair, 2 * pair + 1):
                    start = PIECE * j
                    i, off = start // 128, start % 128
                    if off == 0:
                        slab = fetch(f, l, i)
                    else:
                        slab = jnp.where(
                            lane < 128 - off,
                            spin(fetch(f, l, i), -off),
                            spin(fetch(f, l, i + 1), -off),
                        )
                    out_ref[j, f * 4 + l] = slab
                    start = PIECE * j + 128
                    i, off = start // 128, start % 128
                    target = 64 * (l % 2)
                    tail = spin(fetch(f, l, i), target - off)
                    if off > 64:
                        other = spin(fetch(f, l, i + 1), target - off)
                        tail = jnp.where(lane < target + 128 - off, tail, other)
                    tails.append(tail)
                packed = jnp.where(lane < 64, tails[0], tails[1])
                if f == 2:
                    at = (PIECE * j - 1) % LON
                    i, off = at // 128, at % 128
                    packed = jnp.where(
                        lane == 127,
                        spin(fetch(f, 2 * pair, i), 127 - off),
                        jnp.where(lane == 63, spin(fetch(f, 2 * pair + 1, i), 63 - off), packed),
                    )
                out_ref[j, 12 + f * 2 + pair] = packed


EDGE, THICK, AU, BU, CU, AT, BT, CT, FU, FT = range(10)
BLOCK = 8


def remap_kernel(sigma_ref, inverse_ref, r_ref, wind_ref, temp_ref, s_ref, f_ref, a_ref, lo_ref, hi_ref):
    lane = lax.broadcasted_iota(jnp.int32, (8, 128), 1)
    left = lane < 64
    zero = jnp.zeros((8, 128), F32)

    def turn(x):
        return pltpu.roll(x, 64, axis=1)

    def twice(p, o, odd):
        return jnp.where(left, o, p) if odd else jnp.where(left, p, o)

    def unpack(s, carry):
        ea, eb, ed, fua, fub, fta, ftb = carry
        for l in range(LEV_DEV):
            k = s * LEV_DEV + l
            odd = l % 2
            ua, ta, ha = r_ref[s, l], r_ref[s, 4 + l], r_ref[s, 8 + l]
            packs = [r_ref[s, 12 + 2 * f + l // 2] for f in range(3)]
            turns = [turn(p) for p in packs]
            ub, tb, hb = (o if odd else p for p, o in zip(packs, turns))
            td = twice(packs[1], turns[1], odd)
            hd = twice(packs[2], turns[2], odd)
            pa = ea + 0.5 * ha
            pb = eb + 0.5 * hb
            ra, rb = pltpu.roll(pa, 1, axis=1), pltpu.roll(pb, 1, axis=1)
            la, lb = pltpu.roll(pa, 127, axis=1), pltpu.roll(pb, 127, axis=1)
            wa = jnp.where(lane == 127, lb, la) - jnp.where(lane == 0, rb, ra)
            wb = lb - jnp.where(lane == 0, ra, rb)
            ua = ua - PRESSURE_COEF * wa
            ub = ub - PRESSURE_COEF * wb
            ud = jnp.where(left, ub, turn(ub))
            s_ref[EDGE, k, 0], s_ref[EDGE, k, 1] = ea, ed
            s_ref[THICK, k, 0], s_ref[THICK, k, 1] = ha, hd
            s_ref[FU, k, 0], s_ref[FU, k, 1] = fua, fub
            s_ref[FT, k, 0], s_ref[FT, k, 1] = fta, ftb
            f_ref[0, k, 0], f_ref[0, k, 1] = ua, ud
            f_ref[1, k, 0], f_ref[1, k, 1] = ta, td
            ea, eb, ed = ea + ha, eb + hb, ed + hd
            fua, fub = fua + ha * ua, fub + hd * ud
            fta, ftb = fta + ha * ta, ftb + hd * td
        return ea, eb, ed, fua, fub, fta, ftb

    sums = lax.fori_loop(0, PEERS, unpack, (zero,) * 7)
    surface = (sums[0], sums[2])
    inverse = tuple(1.0 / s for s in surface)

    for m in range(2):
        a_ref[m, 0] = f_ref[m, 0]
        a_ref[m, 1] = 0.5 * (f_ref[m, 0] + f_ref[m, 1])
        a_ref[m, LEVELS - 1] = 0.5 * (f_ref[m, LEVELS - 2] + f_ref[m, LEVELS - 1])
        a_ref[m, LEVELS] = f_ref[m, LEVELS - 1]

    def edges(k, _):
        for m in range(2):
            a_ref[m, k] = (7.0 / 12.0) * (f_ref[m, k - 1] + f_ref[m, k]) - (1.0 / 12.0) * (
                f_ref[m, k - 2] + f_ref[m, k + 1]
            )
        return 0

    lax.fori_loop(2, LEVELS - 1, edges, 0)

    def coefficients(k, _):
        rd = 1.0 / s_ref[THICK, k]
        rd2 = rd * rd
        for m, (pa, pb, pc) in enumerate(((AU, BU, CU), (AT, BT, CT))):
            a0, a1, f = a_ref[m, k], a_ref[m, k + 1], f_ref[m, k]
            c = 6.0 * (f - 0.5 * (a0 + a1))
            s_ref[pa, k] = a0
            s_ref[pb, k] = (0.5 * rd) * (a1 - a0 + c)
            s_ref[pc, k] = (rd2 * (-1.0 / 3.0)) * c
        return 0

    lax.fori_loop(0, LEVELS, coefficients, 0)

    blocks = LEVELS // BLOCK
    bounds = [
        tuple(s * sigma_ref[BLOCK * b - 1] for s in surface) for b in range(1, blocks)
    ]

    def count(k, carry):
        ea, eb = s_ref[EDGE, k, 0], s_ref[EDGE, k, 1]
        out = []
        for (pa, pb), (ca, cb) in zip(bounds, carry):
            out.append((ca + jnp.where(ea <= pa, 1.0, 0.0), cb + jnp.where(eb <= pb, 1.0, 0.0)))
        return tuple(out)

    counts = lax.fori_loop(1, LEVELS, count, tuple((zero, zero) for _ in bounds))
    lo_ref[0] = 0
    hi_ref[blocks - 1] = LEVELS
    for b, (ca, cb) in enumerate(counts):
        lo_ref[b + 1] = jnp.min(jnp.minimum(ca, cb)).astype(jnp.int32)
        hi_ref[b] = jnp.max(jnp.maximum(ca, cb)).astype(jnp.int32) + 1

    def block(b, carry):
        low, high = lo_ref[b], hi_ref[b]
        base = b * BLOCK
        pa = [surface[0] * sigma_ref[base + i] for i in range(BLOCK)]
        pb = [
            surface[1] * jnp.where(left, sigma_ref[base + 2 * i], sigma_ref[base + 2 * i + 1])
            for i in range(BLOCK // 2)
        ]
        places = [(p, 0) for p in pa] + [(p, 1) for p in pb]
        start = []
        for p, part in places:
            start += [s_ref[FU, low, part], s_ref[FT, low, part]]

        def layer(k, sums):
            out = []
            for part in range(2):
                e, d, au, bu, cu, at, bt, ct = (s_ref[plane, k, part] for plane in range(8))
                for n, (p, where) in enumerate(places):
                    if where == part:
                        y = jnp.minimum(jnp.maximum(p - e, 0.0), d)
                        out.append(sums[2 * n] + y * (au + y * (bu + y * cu)))
                        out.append(sums[2 * n + 1] + y * (at + y * (bt + y * ct)))
            return tuple(out)

        mass = lax.fori_loop(low, high, layer, tuple(start))
        following = []
        for m, out_ref in enumerate((wind_ref, temp_ref)):
            last_a, last_b = carry[2 * m], carry[2 * m + 1]
            for i in range(BLOCK):
                here = mass[2 * i + m]
                factor = inverse[0] * inverse_ref[base + i]
                out_ref[base + i, :, 0:128] = (here - last_a) * factor
                last_a = here
            for i in range(BLOCK // 2):
                here = mass[2 * (BLOCK + i) + m]
                turned = turn(here)
                factor = inverse[1] * jnp.where(
                    left, inverse_ref[base + 2 * i], inverse_ref[base + 2 * i + 1]
                )
                value = (here - jnp.where(left, last_b, turned)) * factor
                out_ref[base + 2 * i, :, 128:PIECE] = value[:, 0:TAIL]
                out_ref[base + 2 * i + 1, :, 128:PIECE] = turn(value)[:, 0:TAIL]
                last_b = turned
            following += [last_a, last_b]
        return tuple(following)

    lax.fori_loop(0, blocks, block, (zero,) * 4)


def whole(space=pltpu.VMEM):
    return pl.BlockSpec(memory_space=space)


def local(zonal_wind, merid_wind, thickness, potential_temp, cutoff, sigma_weights):
    band = lax.axis_index("lat").astype(jnp.int32).reshape(1)
    up = [(i, i + 1) for i in range(BANDS - 1)]
    down = [(i + 1, i) for i in range(BANDS - 1)]
    fields = (merid_wind, thickness, potential_temp)
    south = lax.ppermute(jnp.stack([f[:, ROWS - 1] for f in fields]), "lat", up)
    north = lax.ppermute(jnp.stack([f[:, 0] for f in fields]), "lat", down)
    high, low = mode_table()
    outgoing = pl.pallas_call(
        dynamics_kernel,
        name="dynamics",
        out_shape=jax.ShapeDtypeStruct((PEERS, 18, 8, 128), F32),
        in_specs=[whole(pltpu.SMEM)] * 2 + [whole()] * 8,
        out_specs=whole(),
        scratch_shapes=[
            pltpu.VMEM((VEC, LON), F32),
            pltpu.VMEM((VEC, LON), F32),
            pltpu.VMEM((4, LEV_DEV, ROWS, EXT), F32),
            pltpu.VMEM((3, 8, EXT), F32),
            pltpu.VMEM((2, LEV_DEV, ROWS, EXT), F32),
        ],
    )(
        band, cutoff, zonal_wind, merid_wind, thickness, potential_temp, south, north,
        jnp.asarray(high), jnp.asarray(low),
    )
    columns = lax.all_to_all(outgoing, "lev", split_axis=0, concat_axis=0, tiled=True)
    total = jnp.sum(sigma_weights)
    sigma = jnp.cumsum(sigma_weights) / total
    inverse = total / sigma_weights
    shape = jax.ShapeDtypeStruct((LEVELS, ROWS, PIECE), F32)
    return pl.pallas_call(
        remap_kernel,
        name="remap",
        out_shape=(shape, shape),
        in_specs=[whole(pltpu.SMEM)] * 2 + [whole()],
        out_specs=(whole(), whole()),
        scratch_shapes=[
            pltpu.VMEM((10, LEVELS, 2, 8, 128), F32),
            pltpu.VMEM((2, LEVELS, 2, 8, 128), F32),
            pltpu.VMEM((2, LEVELS + 1, 2, 8, 128), F32),
            pltpu.SMEM((LEVELS // BLOCK,), jnp.int32),
            pltpu.SMEM((LEVELS // BLOCK,), jnp.int32),
        ],
    )(sigma, inverse, columns)


def solution(mesh):
    field = P("lev", "lat", None)
    out = P(None, "lat", "lev")
    return jax.shard_map(
        local,
        mesh=mesh,
        in_specs=(field, field, field, field, P(), P()),
        out_specs=(out, out),
        check_vma=False,
    )
```

```python
import functools
import math

import jax
import jax.numpy as jnp
import numpy as np
from jax import lax
from jax.experimental import pallas as pl
from jax.experimental.pallas import tpu as pltpu
from jax.sharding import PartitionSpec as P

F32 = jnp.float32
BF16 = jnp.bfloat16

LON = 2880
EXT = 2944
CHUNKS = EXT // 128
LEVELS = 64
ROWS = 8
LEV_DEV = 4
BANDS = 32
PEERS = 16
PIECE = LON // PEERS
TAIL = PIECE - 128
RADIX = 5
PART = LON // RADIX
POLAR = 16
COURANT = 0.02
PRESSURE_COEF = 0.05


def mode_table():
    j = np.arange(64)
    orders = [[5 * j], [5 * j + 1, 5 * j + 4], [5 * j + 2, 5 * j + 3]]
    r = np.arange(PART)
    columns = []
    for order in orders:
        waves = np.concatenate(order)
        angle = 2.0 * np.pi * ((r[:, None] * waves[None, :]) % LON) / LON
        columns += [np.cos(angle), np.sin(angle)]
    table = np.concatenate(columns, axis=1)
    high = table.astype(np.float32).astype(jnp.bfloat16)
    low = (table - high.astype(np.float64)).astype(np.float32).astype(jnp.bfloat16)
    return np.stack([high, low])


def split(x):
    high = x.astype(BF16)
    low = (x - high.astype(F32)).astype(BF16)
    return high, low


def dot3(x, table_ref, first, count, transposed):
    dims = (((1,), (1,)), ((), ())) if transposed else (((1,), (0,)), ((), ()))
    x_high, x_low = split(x)
    t_high = table_ref[0, :, first : first + count]
    t_low = table_ref[1, :, first : first + count]
    dot = functools.partial(lax.dot_general, dimension_numbers=dims, preferred_element_type=F32)
    return dot(x_high, t_high) + (dot(x_low, t_high) + dot(x_high, t_low))


def spin(x, shift):
    shift = shift % 128
    return x if shift == 0 else pltpu.roll(x, shift, axis=1)


def filter_rows(x, table_ref, limit):
    vec = x[0].shape[0]
    c1, c2 = math.cos(2 * math.pi / 5), math.cos(4 * math.pi / 5)
    s1, s2 = math.sin(2 * math.pi / 5), math.sin(4 * math.pi / 5)
    sum1, dif1 = x[1] + x[4], x[1] - x[4]
    sum2, dif2 = x[2] + x[3], x[2] - x[3]
    z0 = x[0] + sum1 + sum2
    z1 = jnp.concatenate([x[0] + c1 * sum1 + c2 * sum2, s1 * dif1 + s2 * dif2], axis=0)
    z2 = jnp.concatenate([x[0] + c2 * sum1 + c1 * sum2, s2 * dif1 - s1 * dif2], axis=0)
    lane = lax.broadcasted_iota(jnp.int32, (vec, 128), 1)
    half = lane < 64
    slot = jnp.where(half, lane, lane - 64)
    sign = jnp.where(half, 1.0, -1.0).astype(F32)

    wave0 = 5 * slot
    weight0 = jnp.where(wave0 <= limit, jnp.where(wave0 == 0, 1.0 / LON, 2.0 / LON), 0.0)
    spec0 = dot3(z0, table_ref, 0, 128, False) * weight0
    back0 = dot3(spec0, table_ref, 0, 128, True)
    backs = []
    for z, first, low_wave, high_wave in ((z1, 128, 1, 4), (z2, 384, 2, 3)):
        wave = 5 * slot + jnp.where(half, low_wave, high_wave)
        weight = jnp.where(wave <= limit, 2.0 / LON, 0.0)
        flip = weight * sign
        y = dot3(z, table_ref, first, 256, False)
        cc, cs = y[:vec, :128], y[:vec, 128:]
        sc, ss = y[vec:, :128], y[vec:, 128:]
        a = cc - sign * ss
        b = cs + sign * sc
        even = jnp.concatenate([a * weight, b * weight], axis=1)
        odd = jnp.concatenate([b * flip, -(a * flip)], axis=1)
        back = dot3(jnp.concatenate([even, odd], axis=0), table_ref, first, 256, True)
        backs += [back[:vec], back[vec:]]
    e1, o1, e2, o2 = backs
    out = [back0 + e1 + e2]
    p, m = back0 + c1 * e1 + c2 * e2, s1 * o1 + s2 * o2
    r, n = back0 + c2 * e1 + c1 * e2, s2 * o1 - s1 * o2
    return out + [p + m, r + n, r - n, p - m]


def wrapped(last, first, lane):
    return jnp.where(lane < 64, last, jnp.where(lane < 96, spin(first, 64), spin(last, 64)))


def iotas():
    return (
        lax.broadcasted_iota(jnp.int32, (8, 128), 1),
        lax.broadcasted_iota(jnp.int32, (8, 128), 0),
    )


def load_kernel(
    band_ref, u_hbm, v_hbm, h_hbm, t_hbm, table_hbm, cutoff_hbm,
    u_ref, v_ref, h_ref, t_ref, last_ref, first_ref, table_ref, cutoff_ref, sems,
):
    pairs = (
        (u_hbm, u_ref), (v_hbm, v_ref), (cutoff_hbm, cutoff_ref), (table_hbm, table_ref),
        (h_hbm, h_ref), (t_hbm, t_ref),
    )
    copies = [pltpu.make_async_copy(src, dst, sems.at[n]) for n, (src, dst) in enumerate(pairs)]
    for copy in copies:
        copy.start()
    band = band_ref[0]
    bands = POLAR // ROWS
    own = jnp.logical_or(band < bands, band >= BANDS - bands)
    entry = jnp.where(band < bands, band, band - (BANDS - 2 * bands)) * ROWS
    for copy in copies[:4]:
        copy.wait()

    @pl.when(own)
    def _():
        row = lax.broadcasted_iota(jnp.int32, (8, 128), 0)
        limit = jnp.zeros((8, 128), jnp.int32)
        for r in range(ROWS):
            limit = jnp.where(row == r, cutoff_ref[entry + r], limit)
        spans = [slice(PART * q, PART * (q + 1)) for q in range(RADIX)]
        x = [
            jnp.concatenate([ref[:, :, at].reshape(32, PART) for ref in (u_ref, v_ref)], axis=0)
            for at in spans
        ]
        for at, piece in zip(spans, filter_rows(x, table_ref, jnp.concatenate([limit] * 8, axis=0))):
            u_ref[:, :, at] = piece[0:32].reshape(4, 8, PART)
            v_ref[:, :, at] = piece[32:64].reshape(4, 8, PART)

    for f, ref in enumerate((v_ref, h_ref, t_ref)):
        if f:
            copies[f + 3].wait()
        for l in range(LEV_DEV):
            last_ref[f, l : l + 1, :] = ref[l, ROWS - 1 : ROWS, :]
            first_ref[f, l : l + 1, :] = ref[l, 0:1, :]


def advance_kernel(u_ref, v_ref, h_ref, t_ref, part_ref, tail_ref):
    lane, row = iotas()
    fields = (u_ref, v_ref, h_ref, t_ref)
    for l in range(LEV_DEV):
        for f, ref in enumerate(fields):
            tail_ref[f, l, :, 0:64] = ref[l, :, LON - 64 : LON]
            tail_ref[f, l] = wrapped(tail_ref[f, l], ref[l, :, 0:128], lane)

    scale = COURANT * 0.25
    def level(l, _):

        def load(f, i):
            at = slice(128 * i, 128 * (i + 1))
            if i == CHUNKS - 1:
                return tail_ref[f, l]
            return fields[f][l, :, at]

        i = CHUNKS - 1
        u, h = load(0, i), load(2, i)
        q = h * load(3, i)
        before = tuple(spin(z, 1) for z in (u, h, q))
        flux = {}
        state = {}
        for i in range(CHUNKS + 1):
            if i < CHUNKS:
                u, v, h = load(0, i), load(1, i), load(2, i)
                q = h * load(3, i)
                now = tuple(spin(z, 1) for z in (u, h, q))
                ul, hl, ql = (jnp.where(lane == 0, b, n) for b, n in zip(before, now))
                before = now
                face = u + ul
                fh, fq = face * (h + hl), face * (q + ql)
                turned = (spin(fh, -1), spin(fq, -1))
                if i == 0:
                    first = turned
                vp, hp, qp = (pltpu.roll(z, 7, axis=0) for z in (v, h, q))
                wp = v + vp
                gh = jnp.where(row == 7, 0.0, wp * (h + hp))
                gq = jnp.where(row == 7, 0.0, wp * (q + qp))
                gh = gh - pltpu.roll(gh, 1, axis=0) - fh
                gq = gq - pltpu.roll(gq, 1, axis=0) - fq
                state[i] = (h, q, gh, gq)
                flux[i] = turned
            if i >= 1:
                k = i - 1
                nxt = flux[i] if i < CHUNKS else first
                h0, q0, gh0, gq0 = state.pop(k)
                mine = flux.pop(k)
                rh = jnp.where(lane == 127, nxt[0], mine[0])
                rq = jnp.where(lane == 127, nxt[1], mine[1])
                at = slice(128 * k, 128 * (k + 1))
                part_ref[0, l, :, at] = h0 - scale * (rh + gh0)
                part_ref[1, l, :, at] = q0 - scale * (rq + gq0)
        return 0

    lax.fori_loop(0, LEV_DEV, level, 0)


def pack_kernel(
    south_ref, north_ref, first_ref, last_ref, u_ref, part_ref,
    out_ref, halo_ref, edge_ref, flux_ref, n_ref,
):
    lane, row = iotas()
    end = slice(EXT - 128, EXT)
    for f in range(3):
        halo_ref[f, 0:4, 0:LON] = south_ref[f]
        halo_ref[f, 4:8, 0:LON] = north_ref[f]
        edge_ref[f, 0:4, 0:LON] = first_ref[f]
        edge_ref[f, 4:8, 0:LON] = last_ref[f]
        for ref in (halo_ref, edge_ref):
            ref[f, :, end] = wrapped(ref[f, :, end], ref[f, :, 0:128], lane)

    scale = COURANT * 0.25
    sign = jnp.where(row < 4, scale, -scale).astype(F32)
    for i in range(CHUNKS):
        at = slice(128 * i, 128 * (i + 1))
        v, h, t = (halo_ref[f, :, at] for f in range(3))
        w = (v + edge_ref[0, :, at]) * sign
        faces = w * (h + edge_ref[1, :, at]), w * (h * t + edge_ref[1, :, at] * edge_ref[2, :, at])
        for m, face in enumerate(faces):
            for r in range(8):
                flux_ref[m, r, :, at] = face[r : r + 1]

    def finish(l, _):
        for i in range(CHUNKS):
            at = slice(128 * i, 128 * (i + 1))

            def outer(m):
                low = jnp.broadcast_to(flux_ref[m, l, :, at], (8, 128))
                high = jnp.broadcast_to(flux_ref[m, l + 4, :, at], (8, 128))
                return jnp.where(row == 0, low, jnp.where(row == 7, high, 0.0))

            new_h = part_ref[0, l, :, at] + outer(0)
            new_q = part_ref[1, l, :, at] + outer(1)
            if i < CHUNKS - 1:
                n_ref[0, l, :, at] = u_ref[l, :, at]
            n_ref[1, l, :, at] = new_q / new_h
            n_ref[2, l, :, at] = new_h
        n_ref[0, l, :, LON - 64 : LON] = u_ref[l, :, LON - 64 : LON]
        n_ref[0, l, :, end] = wrapped(n_ref[0, l, :, end], u_ref[l, :, 0:128], lane)
        return 0

    lax.fori_loop(0, LEV_DEV, finish, 0)

    def place(f, pair, with_sides):
        def fetch(l, i):
            return n_ref[f, 2 * pair + l, :, 128 * i : 128 * (i + 1)]

        for j in range(PEERS):
            tails = []
            for l in range(2):
                start = PIECE * j
                i, off = start // 128, start % 128
                slab = spin(fetch(l, i), -off)
                if off:
                    slab = jnp.where(lane < 128 - off, slab, spin(fetch(l, i + 1), -off))
                out_ref[j, f * 4 + 2 * pair + l] = slab
                i, off = (start + 128) // 128, (start + 128) % 128
                tail = spin(fetch(l, i), 64 * l - off)
                if off > 64:
                    other = spin(fetch(l, i + 1), 64 * l - off)
                    tail = jnp.where(lane < 64 * l + 128 - off, tail, other)
                tails.append(tail)
            packed = jnp.where(lane < 64, tails[0], tails[1])
            if with_sides:
                at = (PIECE * j - 1) % LON
                i, off = at // 128, at % 128
                packed = jnp.where(
                    lane == 127,
                    spin(fetch(0, i), 127 - off),
                    jnp.where(lane == 63, spin(fetch(1, i), 63 - off), packed),
                )
            out_ref[j, 12 + f * 2 + pair] = packed
        return 0

    lax.fori_loop(0, 4, lambda n, _: place(n // 2, n % 2, False), 0)
    lax.fori_loop(0, 2, lambda n, _: place(2, n, True), 0)


EDGE, AU, BU, CU, FU, AT, BT, CT, FT = range(9)
BLOCK = 8
WINDOW = 10
UNROLL = 2
MARGIN = 1e-5


def remap_kernel(
    sigma_ref, inverse_ref, row_ref, r_ref, wind_hbm, temp_hbm,
    s_ref, d_ref, f_ref, m_ref, x_ref, bound_ref, scalar_ref, wind_ref, temp_ref, sems, bound_sem,
):
    lane, row = iotas()
    left = lane < 64
    even = jnp.logical_or(jnp.logical_and(left, lane != 63), lane == 127)
    zero = jnp.zeros((8, 128), F32)

    def turn(x):
        return pltpu.roll(x, 64, axis=1)

    def unpack(n, carry):
        ea, eb, fua, fub, fta, ftb = carry
        for s in range(2):
            for pair in range(2):
                packs = [r_ref[2 * n + s, 12 + 2 * f + pair] for f in range(3)]
                turns = [turn(p) for p in packs]
                for odd in range(2):
                    l = 2 * pair + odd
                    k = n * 8 + s * 4 + l
                    ua, ta, ha = (r_ref[2 * n + s, 4 * f + l] for f in range(3))
                    ub = turns[0] if odd else packs[0]
                    tb, hb = (
                        jnp.where(even, o, p) if odd else jnp.where(even, p, o)
                        for p, o in zip(packs[1:], turns[1:])
                    )
                    pa = ea + 0.5 * ha
                    pb = eb + 0.5 * hb
                    ra, rb = pltpu.roll(pa, 1, axis=1), pltpu.roll(pb, 1, axis=1)
                    la, lb = pltpu.roll(pa, 127, axis=1), pltpu.roll(pb, 127, axis=1)
                    wa = jnp.where(lane == 127, lb, la) - jnp.where(lane == 0, rb, ra)
                    wb = lb - jnp.where(lane == 0, ra, rb)
                    ua = ua - PRESSURE_COEF * wa
                    ub = ub - PRESSURE_COEF * wb
                    ub = jnp.where(left, ub, turn(ub))
                    s_ref[k, 0, EDGE], s_ref[k, 1, EDGE] = ea, eb
                    d_ref[k, 0], d_ref[k, 1] = ha, hb
                    s_ref[k, 0, FU], s_ref[k, 1, FU] = fua, fub
                    s_ref[k, 0, FT], s_ref[k, 1, FT] = fta, ftb
                    f_ref[0, k, 0], f_ref[0, k, 1] = ua, ub
                    f_ref[1, k, 0], f_ref[1, k, 1] = ta, tb
                    ea, eb = ea + ha, eb + hb
                    fua, fub = fua + ha * ua, fub + hb * ub
                    fta, ftb = fta + ha * ta, ftb + hb * tb
        return ea, eb, fua, fub, fta, ftb

    sums = lax.fori_loop(0, PEERS // 2, unpack, (zero,) * 6)
    surface = sums[:2]
    inverse = tuple(1.0 / s for s in surface)
    for k in range(WINDOW):
        s_ref[LEVELS + k, :, EDGE] = jnp.full((2, 8, 128), 1e30, F32)

    targets = jnp.broadcast_to(row_ref[...], (8, 128))

    def tally(n, counts):
        for j in range(8):
            xa, xb = (s_ref[n * 8 + j, part, EDGE] * inverse[part] for part in range(2))
            x_ref[0, 8 * j : 8 * j + 8, :] = jnp.maximum(xa, xb)
            x_ref[1, 8 * j : 8 * j + 8, :] = jnp.minimum(xa, xb)
        out = []
        for side, best, shift in ((0, jnp.maximum, -MARGIN), (1, jnp.minimum, MARGIN)):
            ref = x_ref.at[side]
            rows = [ref[pl.ds(r, 8, stride=8), :] for r in range(8)]
            while len(rows) > 1:
                rows = [best(p, q) for p, q in zip(rows[::2], rows[1::2])]
            reduce = jnp.max if side == 0 else jnp.min
            edge = reduce(rows[0], axis=1, keepdims=True)
            out.append(counts[side] + jnp.where(edge <= targets + shift, 1.0, 0.0))
        return tuple(out)

    counts = lax.fori_loop(0, LEVELS // 8, tally, (zero, zero))
    low, high = (jnp.sum(c, axis=0, keepdims=True) for c in counts)
    low = jnp.maximum(low - 1.0, 0.0)
    bound_ref[...] = jnp.where(row == 0, low, high).astype(jnp.int32)
    to_scalars = pltpu.make_async_copy(bound_ref, scalar_ref, bound_sem)
    to_scalars.start()

    def middle(m, k):
        return (7.0 / 12.0) * (f_ref[m, k - 1] + f_ref[m, k]) - (1.0 / 12.0) * (
            f_ref[m, k - 2] + f_ref[m, k + 1]
        )

    def layer(k, lower, upper):
        rd = 1.0 / d_ref[k]
        square = rd * rd
        for m, (pa, pb, pc) in enumerate(((AU, BU, CU), (AT, BT, CT))):
            a0, a1, f = lower[m], upper[m], f_ref[m, k]
            rise, rest = f - a0, a1 - f
            s_ref[k, :, pa] = a0
            s_ref[k, :, pb] = rd * (rise + (rise - rest))
            s_ref[k, :, pc] = square * (rest - rise)

    def layers(n, lower):
        for j in range(4):
            k = 1 + 4 * n + j
            upper = tuple(middle(m, k + 1) for m in range(2))
            layer(k, lower, upper)
            lower = upper
        return lower

    last = LEVELS - 1
    second = tuple(0.5 * (f_ref[m, 0] + f_ref[m, 1]) for m in range(2))
    layer(0, tuple(f_ref[m, 0] for m in range(2)), second)
    lower = lax.fori_loop(0, 15, layers, second)
    for k in range(61, LEVELS):
        if k < last - 1:
            upper = tuple(middle(m, k + 1) for m in range(2))
        elif k == last - 1:
            upper = tuple(0.5 * (f_ref[m, last - 1] + f_ref[m, last]) for m in range(2))
        else:
            upper = tuple(f_ref[m, last] for m in range(2))
        layer(k, lower, upper)
        lower = upper

    to_scalars.wait()

    def places(g):
        i = 2 * g
        s0, s1 = sigma_ref[i], sigma_ref[i + 1]
        return (
            (surface[0] * s0, 0),
            (surface[0] * s1, 0),
            (surface[1] * jnp.where(left, s0, s1), 1),
        )

    def begin(points, low):
        return tuple(tuple(s_ref[low, part, plane] for plane in range(9)) for _, part in points)

    def pick(points, k, state):
        values = [[s_ref[k, part, plane] for plane in range(9)] for part in range(2)]
        out = []
        for (p, part), held in zip(points, state):
            inside = p >= values[part][EDGE]
            out.append(tuple(jnp.where(inside, v, h) for v, h in zip(values[part], held)))
        return tuple(out)

    def mass_of(g, points, state):
        slots = (2 * g, 2 * g + 1, LEVELS + g)
        for slot, (p, _), held in zip(slots, points, state):
            y = p - held[EDGE]
            for m, (a, b, c, f) in enumerate(((AU, BU, CU, FU), (AT, BT, CT, FT))):
                m_ref[m, slot] = held[f] + y * (held[a] + y * (held[b] + y * held[c]))

    def pairs(n, _):
        for j in range(UNROLL):
            g = UNROLL * n + j
            points = places(g)
            low = scalar_ref[0, 2 * g]
            state = begin(points, low)
            for k in range(1, WINDOW):
                state = pick(points, low + k, state)
            mass_of(g, points, state)
        for j in range(UNROLL):
            g = UNROLL * n + j
            low, high = scalar_ref[0, 2 * g], scalar_ref[1, 2 * g + 1]

            @pl.when(high - low > WINDOW)
            def _():
                points = places(g)
                state = lax.fori_loop(
                    low + 1, high, functools.partial(pick, points), begin(points, low)
                )
                mass_of(g, points, state)

        return 0

    def leave(b, m):
        ref, hbm = ((wind_ref, wind_hbm), (temp_ref, temp_hbm))[m]
        at = pl.ds(b * BLOCK, BLOCK)
        return pltpu.make_async_copy(ref.at[at], hbm.at[at], sems.at[m, b])

    def block(b, carry):
        lax.fori_loop(b * (BLOCK // 2 // UNROLL), (b + 1) * (BLOCK // 2 // UNROLL), pairs, 0)
        carry = list(carry)
        for m, ref in enumerate((wind_ref, temp_ref)):
            for j in range(BLOCK // 2):
                i = b * BLOCK + 2 * j
                masses = m_ref[m, i], m_ref[m, i + 1]
                tail = m_ref[m, LEVELS + b * (BLOCK // 2) + j]
                turned = turn(tail)
                tails = tail, turned
                for n in range(2):
                    width = inverse_ref[i + n]
                    ref[i + n, :, 0:128] = (masses[n] - carry[2 * m]) * (inverse[0] * width)
                    value = (tails[n] - carry[2 * m + 1]) * (inverse[1] * width)
                    ref[i + n, :, 128:PIECE] = value[:, 0:TAIL]
                    carry[2 * m], carry[2 * m + 1] = masses[n], tails[n]
            leave(b, m).start()
        return tuple(carry)

    lax.fori_loop(0, LEVELS // BLOCK, block, (zero,) * 4)
    for b in range(LEVELS // BLOCK):
        for m in range(2):
            leave(b, m).wait()


VMEM = pltpu.MemorySpace.VMEM


def whole(space=pltpu.VMEM):
    return pl.BlockSpec(memory_space=space)


def keep(x):
    return pltpu.with_memory_space_constraint(x, VMEM)


def local(zonal_wind, merid_wind, thickness, potential_temp, cutoff, sigma_weights):
    band = lax.axis_index("lat").astype(jnp.int32).reshape(1)
    up = [(i, i + 1) for i in range(BANDS - 1)]
    down = [(i + 1, i) for i in range(BANDS - 1)]
    inputs = (zonal_wind, merid_wind, thickness, potential_temp)
    edge = pltpu.VMEM((3, LEV_DEV, LON), F32)
    field = pltpu.VMEM((LEV_DEV, ROWS, LON), F32)
    table = mode_table()
    *fields, last, first = pl.pallas_call(
        load_kernel,
        name="load",
        compiler_params=pltpu.CompilerParams(vmem_limit_bytes=16 << 20),
        out_shape=(field,) * 4 + (edge,) * 2,
        in_specs=[whole(pltpu.SMEM)] + [whole(pltpu.HBM)] * 6,
        out_specs=(whole(),) * 6,
        scratch_shapes=[
            pltpu.VMEM(table.shape, BF16),
            pltpu.SMEM(cutoff.shape, jnp.int32),
            pltpu.SemaphoreType.DMA((6,)),
        ],
    )(
        band,
        *(
            pltpu.with_memory_space_constraint(x, pltpu.HBM)
            for x in (*inputs, jnp.asarray(table), cutoff)
        ),
    )
    fields = [keep(x) for x in fields]
    south = lax.ppermute(last, "lat", up)
    north = lax.ppermute(first, "lat", down)
    (part,) = pl.pallas_call(
        advance_kernel,
        name="advance",
        compiler_params=pltpu.CompilerParams(vmem_limit_bytes=16 << 20),
        out_shape=(pltpu.VMEM((2, LEV_DEV, ROWS, EXT), F32),),
        in_specs=[whole()] * 4,
        out_specs=(whole(),),
        scratch_shapes=[pltpu.VMEM((4, LEV_DEV, ROWS, 128), F32)],
    )(*fields)
    outgoing = pl.pallas_call(
        pack_kernel,
        name="pack",
        compiler_params=pltpu.CompilerParams(vmem_limit_bytes=16 << 20),
        out_shape=pltpu.VMEM((PEERS, 18, 8, 128), F32),
        in_specs=[whole()] * 6,
        out_specs=whole(),
        scratch_shapes=[
            pltpu.VMEM((3, 8, EXT), F32),
            pltpu.VMEM((3, 8, EXT), F32),
            pltpu.VMEM((2, 8, 1, EXT), F32),
            pltpu.VMEM((3, LEV_DEV, ROWS, EXT), F32),
        ],
    )(*map(keep, (south, north, first, last)), fields[0], keep(part))
    columns = lax.all_to_all(outgoing, "lev", split_axis=0, concat_axis=0, tiled=True)
    total = jnp.sum(sigma_weights)
    sigma = jnp.cumsum(sigma_weights) / total
    inverse = total / sigma_weights
    sigma_row = jnp.pad(sigma, (0, 128 - LEVELS), constant_values=2.0).reshape(1, 128)
    shape = jax.ShapeDtypeStruct((LEVELS, ROWS, PIECE), F32)
    return pl.pallas_call(
        remap_kernel,
        name="remap",
        compiler_params=pltpu.CompilerParams(vmem_limit_bytes=24 << 20),
        out_shape=(shape, shape),
        in_specs=[whole(pltpu.SMEM)] * 2 + [whole()] * 2,
        out_specs=(whole(pltpu.HBM), whole(pltpu.HBM)),
        scratch_shapes=[
            pltpu.VMEM((LEVELS + WINDOW, 2, 9, 8, 128), F32),
            pltpu.VMEM((LEVELS, 2, 8, 128), F32),
            pltpu.VMEM((2, LEVELS, 2, 8, 128), F32),
            pltpu.VMEM((2, LEVELS + LEVELS // 2, 8, 128), F32),
            pltpu.VMEM((2, 64, 128), F32),
            pltpu.VMEM((8, 128), jnp.int32),
            pltpu.SMEM((8, 128), jnp.int32),
            pltpu.VMEM((LEVELS, ROWS, PIECE), F32),
            pltpu.VMEM((LEVELS, ROWS, PIECE), F32),
            pltpu.SemaphoreType.DMA((2, LEVELS // BLOCK)),
            pltpu.SemaphoreType.DMA,
        ],
    )(sigma, inverse, sigma_row, keep(columns))


def solution(mesh):
    field = P("lev", "lat", None)
    out = P(None, "lat", "lev")
    return jax.shard_map(
        local,
        mesh=mesh,
        in_specs=(field, field, field, field, P(), P()),
        out_specs=(out, out),
        check_vma=False,
    )
```

```python
import functools
import math

import jax
import jax.numpy as jnp
import numpy as np
from jax import lax
from jax.experimental import pallas as pl
from jax.experimental.pallas import tpu as pltpu
from jax.sharding import PartitionSpec as P

F32 = jnp.float32
BF16 = jnp.bfloat16

LON = 2880
EXT = 2944
CHUNKS = EXT // 128
LEVELS = 64
ROWS = 8
LEV_DEV = 4
BANDS = 32
PEERS = 16
PIECE = LON // PEERS
TAIL = PIECE - 128
RADIX = 5
PART = LON // RADIX
POLAR = 16
COURANT = 0.02
PRESSURE_COEF = 0.05


def mode_table():
    j = np.arange(64)
    orders = [[5 * j], [5 * j + 1, 5 * j + 4], [5 * j + 2, 5 * j + 3]]
    r = np.arange(PART)
    columns = []
    for order in orders:
        waves = np.concatenate(order)
        angle = 2.0 * np.pi * ((r[:, None] * waves[None, :]) % LON) / LON
        columns += [np.cos(angle), np.sin(angle)]
    table = np.concatenate(columns, axis=1)
    high = table.astype(np.float32).astype(jnp.bfloat16)
    low = (table - high.astype(np.float64)).astype(np.float32).astype(jnp.bfloat16)
    return np.stack([high, low])


def split(x):
    high = x.astype(BF16)
    low = (x - high.astype(F32)).astype(BF16)
    return high, low


def dot3(x, table_ref, first, count, transposed):
    dims = (((1,), (1,)), ((), ())) if transposed else (((1,), (0,)), ((), ()))
    x_high, x_low = split(x)
    t_high = table_ref[0, :, first : first + count]
    t_low = table_ref[1, :, first : first + count]
    dot = functools.partial(lax.dot_general, dimension_numbers=dims, preferred_element_type=F32)
    return dot(x_high, t_high) + (dot(x_low, t_high) + dot(x_high, t_low))


def spin(x, shift):
    shift = shift % 128
    return x if shift == 0 else pltpu.roll(x, shift, axis=1)


def filter_rows(x, table_ref, limit):
    vec = x[0].shape[0]
    c1, c2 = math.cos(2 * math.pi / 5), math.cos(4 * math.pi / 5)
    s1, s2 = math.sin(2 * math.pi / 5), math.sin(4 * math.pi / 5)
    sum1, dif1 = x[1] + x[4], x[1] - x[4]
    sum2, dif2 = x[2] + x[3], x[2] - x[3]
    z0 = x[0] + sum1 + sum2
    z1 = jnp.concatenate([x[0] + c1 * sum1 + c2 * sum2, s1 * dif1 + s2 * dif2], axis=0)
    z2 = jnp.concatenate([x[0] + c2 * sum1 + c1 * sum2, s2 * dif1 - s1 * dif2], axis=0)
    lane = lax.broadcasted_iota(jnp.int32, (vec, 128), 1)
    half = lane < 64
    slot = jnp.where(half, lane, lane - 64)
    sign = jnp.where(half, 1.0, -1.0).astype(F32)

    wave0 = 5 * slot
    weight0 = jnp.where(wave0 <= limit, jnp.where(wave0 == 0, 1.0 / LON, 2.0 / LON), 0.0)
    spec0 = dot3(z0, table_ref, 0, 128, False) * weight0
    back0 = dot3(spec0, table_ref, 0, 128, True)
    backs = []
    for z, first, low_wave, high_wave in ((z1, 128, 1, 4), (z2, 384, 2, 3)):
        wave = 5 * slot + jnp.where(half, low_wave, high_wave)
        weight = jnp.where(wave <= limit, 2.0 / LON, 0.0)
        flip = weight * sign
        y = dot3(z, table_ref, first, 256, False)
        cc, cs = y[:vec, :128], y[:vec, 128:]
        sc, ss = y[vec:, :128], y[vec:, 128:]
        a = cc - sign * ss
        b = cs + sign * sc
        even = jnp.concatenate([a * weight, b * weight], axis=1)
        odd = jnp.concatenate([b * flip, -(a * flip)], axis=1)
        back = dot3(jnp.concatenate([even, odd], axis=0), table_ref, first, 256, True)
        backs += [back[:vec], back[vec:]]
    e1, o1, e2, o2 = backs
    out = [back0 + e1 + e2]
    p, m = back0 + c1 * e1 + c2 * e2, s1 * o1 + s2 * o2
    r, n = back0 + c2 * e1 + c1 * e2, s2 * o1 - s1 * o2
    return out + [p + m, r + n, r - n, p - m]


def wrapped(last, first, lane):
    return jnp.where(lane < 64, last, jnp.where(lane < 96, spin(first, 64), spin(last, 64)))


def iotas():
    return (
        lax.broadcasted_iota(jnp.int32, (8, 128), 1),
        lax.broadcasted_iota(jnp.int32, (8, 128), 0),
    )


def load_kernel(
    band_ref, u_hbm, v_hbm, h_hbm, t_hbm, table_hbm, cutoff_hbm,
    u_ref, v_ref, h_ref, t_ref, last_ref, first_ref, table_ref, cutoff_ref, sems,
):
    pairs = (
        (u_hbm, u_ref), (v_hbm, v_ref), (cutoff_hbm, cutoff_ref), (table_hbm, table_ref),
        (h_hbm, h_ref), (t_hbm, t_ref),
    )
    copies = [pltpu.make_async_copy(src, dst, sems.at[n]) for n, (src, dst) in enumerate(pairs)]
    for copy in copies:
        copy.start()
    band = band_ref[0]
    bands = POLAR // ROWS
    own = jnp.logical_or(band < bands, band >= BANDS - bands)
    entry = jnp.where(band < bands, band, band - (BANDS - 2 * bands)) * ROWS
    for copy in copies[:4]:
        copy.wait()

    @pl.when(own)
    def _():
        row = lax.broadcasted_iota(jnp.int32, (8, 128), 0)
        limit = jnp.zeros((8, 128), jnp.int32)
        for r in range(ROWS):
            limit = jnp.where(row == r, cutoff_ref[entry + r], limit)
        spans = [slice(PART * q, PART * (q + 1)) for q in range(RADIX)]
        x = [
            jnp.concatenate([ref[:, :, at].reshape(32, PART) for ref in (u_ref, v_ref)], axis=0)
            for at in spans
        ]
        for at, piece in zip(spans, filter_rows(x, table_ref, jnp.concatenate([limit] * 8, axis=0))):
            u_ref[:, :, at] = piece[0:32].reshape(4, 8, PART)
            v_ref[:, :, at] = piece[32:64].reshape(4, 8, PART)

    for f, ref in enumerate((v_ref, h_ref, t_ref)):
        if f:
            copies[f + 3].wait()
        for l in range(LEV_DEV):
            last_ref[f, l : l + 1, :] = ref[l, ROWS - 1 : ROWS, :]
            first_ref[f, l : l + 1, :] = ref[l, 0:1, :]


def place(slot_ref, fetch, lane, with_sides):
    for j in range(PEERS):
        tails = []
        for l in range(2):
            start = PIECE * j
            i, off = start // 128, start % 128
            slab = spin(fetch(l, i), -off)
            if off:
                slab = jnp.where(lane < 128 - off, slab, spin(fetch(l, i + 1), -off))
            slot_ref[j, l] = slab
            i, off = (start + 128) // 128, (start + 128) % 128
            tail = spin(fetch(l, i), 64 * l - off)
            if off > 64:
                other = spin(fetch(l, i + 1), 64 * l - off)
                tail = jnp.where(lane < 64 * l + 128 - off, tail, other)
            tails.append(tail)
        packed = jnp.where(lane < 64, tails[0], tails[1])
        if with_sides:
            at = (PIECE * j - 1) % LON
            i, off = at // 128, at % 128
            packed = jnp.where(
                lane == 127,
                spin(fetch(0, i), 127 - off),
                jnp.where(lane == 63, spin(fetch(1, i), 63 - off), packed),
            )
        slot_ref[j, 2] = packed


def send(slots_ref, out_hbm, sems, slot, group):
    dst = out_hbm.at[:, pl.ds(group, 3)]
    return pltpu.make_async_copy(slots_ref.at[slot], dst, sems.at[slot])


def advance_kernel(u_ref, v_ref, h_ref, t_ref, part_ref, out_hbm, tail_ref, slots_ref, sems):
    lane, row = iotas()
    fields = (u_ref, v_ref, h_ref, t_ref)
    for l in range(LEV_DEV):
        for f, ref in enumerate(fields):
            tail_ref[f, l, :, 0:64] = ref[l, :, LON - 64 : LON]
            tail_ref[f, l] = wrapped(tail_ref[f, l], ref[l, :, 0:128], lane)

    def put(pair, _):
        def fetch(l, i):
            if i == CHUNKS - 1:
                return tail_ref[0, 2 * pair + l]
            return u_ref[2 * pair + l, :, 128 * i : 128 * (i + 1)]

        place(slots_ref.at[pair], fetch, lane, False)
        send(slots_ref, out_hbm, sems, pair, 3 * pair).start()
        return 0

    lax.fori_loop(0, 2, put, 0)

    scale = COURANT * 0.25
    def level(l, _):

        def load(f, i):
            at = slice(128 * i, 128 * (i + 1))
            if i == CHUNKS - 1:
                return tail_ref[f, l]
            return fields[f][l, :, at]

        i = CHUNKS - 1
        u, h = load(0, i), load(2, i)
        q = h * load(3, i)
        before = tuple(spin(z, 1) for z in (u, h, q))
        flux = {}
        state = {}
        for i in range(CHUNKS + 1):
            if i < CHUNKS:
                u, v, h = load(0, i), load(1, i), load(2, i)
                q = h * load(3, i)
                now = tuple(spin(z, 1) for z in (u, h, q))
                ul, hl, ql = (jnp.where(lane == 0, b, n) for b, n in zip(before, now))
                before = now
                face = u + ul
                fh, fq = face * (h + hl), face * (q + ql)
                turned = (spin(fh, -1), spin(fq, -1))
                if i == 0:
                    first = turned
                vp, hp, qp = (pltpu.roll(z, 7, axis=0) for z in (v, h, q))
                wp = v + vp
                gh = jnp.where(row == 7, 0.0, wp * (h + hp))
                gq = jnp.where(row == 7, 0.0, wp * (q + qp))
                gh = gh - pltpu.roll(gh, 1, axis=0) - fh
                gq = gq - pltpu.roll(gq, 1, axis=0) - fq
                state[i] = (h, q, gh, gq)
                flux[i] = turned
            if i >= 1:
                k = i - 1
                nxt = flux[i] if i < CHUNKS else first
                h0, q0, gh0, gq0 = state.pop(k)
                mine = flux.pop(k)
                rh = jnp.where(lane == 127, nxt[0], mine[0])
                rq = jnp.where(lane == 127, nxt[1], mine[1])
                at = slice(128 * k, 128 * (k + 1))
                part_ref[0, l, :, at] = h0 - scale * (rh + gh0)
                part_ref[1, l, :, at] = q0 - scale * (rq + gq0)
        return 0

    lax.fori_loop(0, LEV_DEV, level, 0)
    for pair in range(2):
        send(slots_ref, out_hbm, sems, pair, 3 * pair).wait()


def pack_kernel(
    south_ref, north_ref, first_ref, last_ref, part_ref, wind_hbm,
    out_hbm, halo_ref, edge_ref, flux_ref, n_ref, slots_ref, sems,
):
    lane, row = iotas()
    end = slice(EXT - 128, EXT)
    for f in range(3):
        halo_ref[f, 0:4, 0:LON] = south_ref[f]
        halo_ref[f, 4:8, 0:LON] = north_ref[f]
        edge_ref[f, 0:4, 0:LON] = first_ref[f]
        edge_ref[f, 4:8, 0:LON] = last_ref[f]
        for ref in (halo_ref, edge_ref):
            ref[f, :, end] = wrapped(ref[f, :, end], ref[f, :, 0:128], lane)

    scale = COURANT * 0.25
    sign = jnp.where(row < 4, scale, -scale).astype(F32)
    for i in range(CHUNKS):
        at = slice(128 * i, 128 * (i + 1))
        v, h, t = (halo_ref[f, :, at] for f in range(3))
        w = (v + edge_ref[0, :, at]) * sign
        faces = w * (h + edge_ref[1, :, at]), w * (h * t + edge_ref[1, :, at] * edge_ref[2, :, at])
        for m, face in enumerate(faces):
            for r in range(8):
                flux_ref[m, r, :, at] = face[r : r + 1]

    def finish(l, _):
        for i in range(CHUNKS):
            at = slice(128 * i, 128 * (i + 1))

            def outer(m):
                low = jnp.broadcast_to(flux_ref[m, l, :, at], (8, 128))
                high = jnp.broadcast_to(flux_ref[m, l + 4, :, at], (8, 128))
                return jnp.where(row == 0, low, jnp.where(row == 7, high, 0.0))

            new_h = part_ref[0, l, :, at] + outer(0)
            new_q = part_ref[1, l, :, at] + outer(1)
            n_ref[0, l, :, at] = new_q / new_h
            n_ref[1, l, :, at] = new_h
        return 0

    lax.fori_loop(0, LEV_DEV, finish, 0)

    def put(pair, f):
        def fetch(l, i):
            return n_ref[f - 1, 2 * pair + l, :, 128 * i : 128 * (i + 1)]

        slot = 2 * (f - 1) + pair
        place(slots_ref.at[slot], fetch, lane, f == 2)
        send(slots_ref, out_hbm, sems, slot, 6 * f + 3 * pair).start()
        return 0

    for f in (1, 2):
        lax.fori_loop(0, 2, lambda pair, _, f=f: put(pair, f), 0)
    for f in (1, 2):
        for pair in range(2):
            send(slots_ref, out_hbm, sems, 2 * (f - 1) + pair, 6 * f + 3 * pair).wait()


EDGE, AU, BU, CU, FU, AT, BT, CT, FT = range(9)
BLOCK = 8
WINDOW = 10
UNROLL = 2
MARGIN = 1e-5


def remap_kernel(
    sigma_ref, inverse_ref, row_ref, r_ref, wind_hbm, temp_hbm,
    s_ref, d_ref, f_ref, m_ref, x_ref, y_ref, bound_ref, scalar_ref, wind_ref, temp_ref, sems, bound_sem,
):
    lane, row = iotas()
    left = lane < 64
    even = jnp.logical_or(jnp.logical_and(left, lane != 63), lane == 127)
    zero = jnp.zeros((8, 128), F32)

    def turn(x):
        return pltpu.roll(x, 64, axis=1)

    def unpack(n, carry):
        ea, eb, fua, fub, fta, ftb = carry
        for s in range(2):
            for pair in range(2):
                packs = [r_ref[2 * n + s, 6 * f + 3 * pair + 2] for f in range(3)]
                turns = [turn(p) for p in packs]
                for odd in range(2):
                    l = 2 * pair + odd
                    k = n * 8 + s * 4 + l
                    ua, ta, ha = (r_ref[2 * n + s, 6 * f + 3 * pair + odd] for f in range(3))
                    ub = turns[0] if odd else packs[0]
                    tb, hb = (
                        jnp.where(even, o, p) if odd else jnp.where(even, p, o)
                        for p, o in zip(packs[1:], turns[1:])
                    )
                    pa = ea + 0.5 * ha
                    pb = eb + 0.5 * hb
                    ra, rb = pltpu.roll(pa, 1, axis=1), pltpu.roll(pb, 1, axis=1)
                    la, lb = pltpu.roll(pa, 127, axis=1), pltpu.roll(pb, 127, axis=1)
                    wa = jnp.where(lane == 127, lb, la) - jnp.where(lane == 0, rb, ra)
                    wb = lb - jnp.where(lane == 0, ra, rb)
                    ua = ua - PRESSURE_COEF * wa
                    ub = ub - PRESSURE_COEF * wb
                    ub = jnp.where(left, ub, turn(ub))
                    s_ref[k, 0, EDGE], s_ref[k, 1, EDGE] = ea, eb
                    d_ref[k, 0], d_ref[k, 1] = ha, hb
                    s_ref[k, 0, FU], s_ref[k, 1, FU] = fua, fub
                    s_ref[k, 0, FT], s_ref[k, 1, FT] = fta, ftb
                    f_ref[0, k, 0], f_ref[0, k, 1] = ua, ub
                    f_ref[1, k, 0], f_ref[1, k, 1] = ta, tb
                    ea, eb = ea + ha, eb + hb
                    fua, fub = fua + ha * ua, fub + hb * ub
                    fta, ftb = fta + ha * ta, ftb + hb * tb
        return ea, eb, fua, fub, fta, ftb

    sums = lax.fori_loop(0, PEERS // 2, unpack, (zero,) * 6)
    surface = sums[:2]
    inverse = tuple(1.0 / s for s in surface)
    for k in range(WINDOW):
        s_ref[LEVELS + k, :, EDGE] = jnp.full((2, 8, 128), 1e30, F32)

    targets = jnp.broadcast_to(row_ref[...], (8, 128))

    def tally(n, _):
        for j in range(8):
            xa, xb = (s_ref[n * 8 + j, part, EDGE] * inverse[part] for part in range(2))
            x_ref[0, 8 * j : 8 * j + 8, :] = jnp.maximum(xa, xb)
            x_ref[1, 8 * j : 8 * j + 8, :] = jnp.minimum(xa, xb)
        for side, best in ((0, jnp.maximum), (1, jnp.minimum)):
            ref = x_ref.at[side]
            rows = [ref[pl.ds(r, 8, stride=8), :] for r in range(8)]
            while len(rows) > 1:
                rows = [best(p, q) for p, q in zip(rows[::2], rows[1::2])]
            y_ref[side, n] = rows[0]
        return 0

    lax.fori_loop(0, LEVELS // 8, tally, 0)
    counts = []
    for side, reduce, shift in ((0, jnp.max, -MARGIN), (1, jnp.min, MARGIN)):
        ends = [reduce(y_ref[side, n], axis=1, keepdims=True) for n in range(LEVELS // 8)]
        counts.append(sum(jnp.where(e <= targets + shift, 1.0, 0.0) for e in ends))
    low, high = (jnp.sum(c, axis=0, keepdims=True) for c in counts)
    low = jnp.maximum(low - 1.0, 0.0)
    bound_ref[...] = jnp.where(row == 0, low, high).astype(jnp.int32)
    to_scalars = pltpu.make_async_copy(bound_ref, scalar_ref, bound_sem)
    to_scalars.start()

    def middle(m, k):
        return (7.0 / 12.0) * (f_ref[m, k - 1] + f_ref[m, k]) - (1.0 / 12.0) * (
            f_ref[m, k - 2] + f_ref[m, k + 1]
        )

    def layer(k, lower, upper):
        rd = 1.0 / d_ref[k]
        square = rd * rd
        for m, (pa, pb, pc) in enumerate(((AU, BU, CU), (AT, BT, CT))):
            a0, a1, f = lower[m], upper[m], f_ref[m, k]
            rise, rest = f - a0, a1 - f
            s_ref[k, :, pa] = a0
            s_ref[k, :, pb] = rd * (rise + (rise - rest))
            s_ref[k, :, pc] = square * (rest - rise)

    def layers(n, lower):
        for j in range(4):
            k = 1 + 4 * n + j
            upper = tuple(middle(m, k + 1) for m in range(2))
            layer(k, lower, upper)
            lower = upper
        return lower

    last = LEVELS - 1
    second = tuple(0.5 * (f_ref[m, 0] + f_ref[m, 1]) for m in range(2))
    layer(0, tuple(f_ref[m, 0] for m in range(2)), second)
    lower = lax.fori_loop(0, 15, layers, second)
    for k in range(61, LEVELS):
        if k < last - 1:
            upper = tuple(middle(m, k + 1) for m in range(2))
        elif k == last - 1:
            upper = tuple(0.5 * (f_ref[m, last - 1] + f_ref[m, last]) for m in range(2))
        else:
            upper = tuple(f_ref[m, last] for m in range(2))
        layer(k, lower, upper)
        lower = upper

    to_scalars.wait()

    def places(g):
        i = 2 * g
        s0, s1 = sigma_ref[i], sigma_ref[i + 1]
        return (
            (surface[0] * s0, 0),
            (surface[0] * s1, 0),
            (surface[1] * jnp.where(left, s0, s1), 1),
        )

    def begin(points, low):
        return tuple(tuple(s_ref[low, part, plane] for plane in range(9)) for _, part in points)

    def pick(points, k, state):
        values = [[s_ref[k, part, plane] for plane in range(9)] for part in range(2)]
        out = []
        for (p, part), held in zip(points, state):
            inside = p >= values[part][EDGE]
            out.append(tuple(jnp.where(inside, v, h) for v, h in zip(values[part], held)))
        return tuple(out)

    def mass_of(g, points, state):
        slots = (2 * g, 2 * g + 1, LEVELS + g)
        for slot, (p, _), held in zip(slots, points, state):
            y = p - held[EDGE]
            for m, (a, b, c, f) in enumerate(((AU, BU, CU, FU), (AT, BT, CT, FT))):
                m_ref[m, slot] = held[f] + y * (held[a] + y * (held[b] + y * held[c]))

    def pairs(n, _):
        for j in range(UNROLL):
            g = UNROLL * n + j
            points = places(g)
            low = scalar_ref[0, 2 * g]
            state = begin(points, low)
            for k in range(1, WINDOW):
                state = pick(points, low + k, state)
            mass_of(g, points, state)
        for j in range(UNROLL):
            g = UNROLL * n + j
            low, high = scalar_ref[0, 2 * g], scalar_ref[1, 2 * g + 1]

            @pl.when(high - low > WINDOW)
            def _():
                points = places(g)
                state = lax.fori_loop(
                    low + 1, high, functools.partial(pick, points), begin(points, low)
                )
                mass_of(g, points, state)

        return 0

    def leave(b, m):
        ref, hbm = ((wind_ref, wind_hbm), (temp_ref, temp_hbm))[m]
        at = pl.ds(b * BLOCK, BLOCK)
        return pltpu.make_async_copy(ref.at[at], hbm.at[at], sems.at[m, b])

    def block(b, carry):
        lax.fori_loop(b * (BLOCK // 2 // UNROLL), (b + 1) * (BLOCK // 2 // UNROLL), pairs, 0)
        carry = list(carry)
        for m, ref in enumerate((wind_ref, temp_ref)):
            for j in range(BLOCK // 2):
                i = b * BLOCK + 2 * j
                masses = m_ref[m, i], m_ref[m, i + 1]
                tail = m_ref[m, LEVELS + b * (BLOCK // 2) + j]
                turned = turn(tail)
                tails = tail, turned
                for n in range(2):
                    width = inverse_ref[i + n]
                    ref[i + n, :, 0:128] = (masses[n] - carry[2 * m]) * (inverse[0] * width)
                    value = (tails[n] - carry[2 * m + 1]) * (inverse[1] * width)
                    ref[i + n, :, 128:PIECE] = value[:, 0:TAIL]
                    carry[2 * m], carry[2 * m + 1] = masses[n], tails[n]
            leave(b, m).start()
        return tuple(carry)

    lax.fori_loop(0, LEVELS // BLOCK, block, (zero,) * 4)
    for b in range(LEVELS // BLOCK):
        for m in range(2):
            leave(b, m).wait()


VMEM = pltpu.MemorySpace.VMEM


def whole(space=pltpu.VMEM):
    return pl.BlockSpec(memory_space=space)


def keep(x):
    return pltpu.with_memory_space_constraint(x, VMEM)


def local(zonal_wind, merid_wind, thickness, potential_temp, cutoff, sigma_weights):
    band = lax.axis_index("lat").astype(jnp.int32).reshape(1)
    up = [(i, i + 1) for i in range(BANDS - 1)]
    down = [(i + 1, i) for i in range(BANDS - 1)]
    inputs = (zonal_wind, merid_wind, thickness, potential_temp)
    edge = pltpu.VMEM((3, LEV_DEV, LON), F32)
    field = pltpu.VMEM((LEV_DEV, ROWS, LON), F32)
    table = mode_table()
    *fields, last, first = pl.pallas_call(
        load_kernel,
        name="load",
        compiler_params=pltpu.CompilerParams(vmem_limit_bytes=16 << 20),
        out_shape=(field,) * 4 + (edge,) * 2,
        in_specs=[whole(pltpu.SMEM)] + [whole(pltpu.HBM)] * 6,
        out_specs=(whole(),) * 6,
        scratch_shapes=[
            pltpu.VMEM(table.shape, BF16),
            pltpu.SMEM(cutoff.shape, jnp.int32),
            pltpu.SemaphoreType.DMA((6,)),
        ],
    )(
        band,
        *(
            pltpu.with_memory_space_constraint(x, pltpu.HBM)
            for x in (*inputs, jnp.asarray(table), cutoff)
        ),
    )
    fields = [keep(x) for x in fields]
    south = lax.ppermute(last, "lat", up)
    north = lax.ppermute(first, "lat", down)
    window = jax.ShapeDtypeStruct((PEERS, 18, 8, 128), F32)
    slot = (PEERS, 3, 8, 128)
    part, winds = pl.pallas_call(
        advance_kernel,
        name="advance",
        compiler_params=pltpu.CompilerParams(vmem_limit_bytes=16 << 20),
        out_shape=(pltpu.VMEM((2, LEV_DEV, ROWS, EXT), F32), window),
        in_specs=[whole()] * 4,
        out_specs=(whole(), whole(pltpu.HBM)),
        scratch_shapes=[
            pltpu.VMEM((4, LEV_DEV, ROWS, 128), F32),
            pltpu.VMEM((2, *slot), F32),
            pltpu.SemaphoreType.DMA((2,)),
        ],
    )(*fields)
    outgoing = pl.pallas_call(
        pack_kernel,
        name="pack",
        compiler_params=pltpu.CompilerParams(vmem_limit_bytes=16 << 20),
        out_shape=window,
        input_output_aliases={5: 0},
        in_specs=[whole()] * 5 + [whole(pltpu.HBM)],
        out_specs=whole(pltpu.HBM),
        scratch_shapes=[
            pltpu.VMEM((3, 8, EXT), F32),
            pltpu.VMEM((3, 8, EXT), F32),
            pltpu.VMEM((2, 8, 1, EXT), F32),
            pltpu.VMEM((2, LEV_DEV, ROWS, EXT), F32),
            pltpu.VMEM((4, *slot), F32),
            pltpu.SemaphoreType.DMA((4,)),
        ],
    )(*map(keep, (south, north, first, last, part)), winds)
    columns = lax.all_to_all(outgoing, "lev", split_axis=0, concat_axis=0, tiled=True)
    total = jnp.sum(sigma_weights)
    sigma = jnp.cumsum(sigma_weights) / total
    inverse = total / sigma_weights
    sigma_row = jnp.pad(sigma, (0, 128 - LEVELS), constant_values=2.0).reshape(1, 128)
    shape = jax.ShapeDtypeStruct((LEVELS, ROWS, PIECE), F32)
    return pl.pallas_call(
        remap_kernel,
        name="remap",
        compiler_params=pltpu.CompilerParams(vmem_limit_bytes=24 << 20),
        out_shape=(shape, shape),
        in_specs=[whole(pltpu.SMEM)] * 2 + [whole()] * 2,
        out_specs=(whole(pltpu.HBM), whole(pltpu.HBM)),
        scratch_shapes=[
            pltpu.VMEM((LEVELS + WINDOW, 2, 9, 8, 128), F32),
            pltpu.VMEM((LEVELS, 2, 8, 128), F32),
            pltpu.VMEM((2, LEVELS, 2, 8, 128), F32),
            pltpu.VMEM((2, LEVELS + LEVELS // 2, 8, 128), F32),
            pltpu.VMEM((2, 64, 128), F32),
            pltpu.VMEM((2, LEVELS // 8, 8, 128), F32),
            pltpu.VMEM((8, 128), jnp.int32),
            pltpu.SMEM((8, 128), jnp.int32),
            pltpu.VMEM((LEVELS, ROWS, PIECE), F32),
            pltpu.VMEM((LEVELS, ROWS, PIECE), F32),
            pltpu.SemaphoreType.DMA((2, LEVELS // BLOCK)),
            pltpu.SemaphoreType.DMA,
        ],
    )(sigma, inverse, sigma_row, keep(columns))


def solution(mesh):
    field = P("lev", "lat", None)
    out = P(None, "lat", "lev")
    return jax.shard_map(
        local,
        mesh=mesh,
        in_specs=(field, field, field, field, P(), P()),
        out_specs=(out, out),
        check_vma=False,
    )
```

```python
import functools
import math

import jax
import jax.numpy as jnp
import numpy as np
from jax import lax
from jax.experimental import pallas as pl
from jax.experimental.pallas import tpu as pltpu
from jax.sharding import PartitionSpec as P

F32 = jnp.float32
BF16 = jnp.bfloat16

LON = 2880
EXT = 2944
CHUNKS = EXT // 128
LEVELS = 64
ROWS = 8
LEV_DEV = 4
BANDS = 32
PEERS = 16
PIECE = LON // PEERS
TAIL = PIECE - 128
RADIX = 5
PART = LON // RADIX
POLAR = 16
COURANT = 0.02
PRESSURE_COEF = 0.05


def mode_table():
    j = np.arange(64)
    orders = [[5 * j], [5 * j + 1, 5 * j + 4], [5 * j + 2, 5 * j + 3]]
    r = np.arange(PART)
    columns = []
    for order in orders:
        waves = np.concatenate(order)
        angle = 2.0 * np.pi * ((r[:, None] * waves[None, :]) % LON) / LON
        columns += [np.cos(angle), np.sin(angle)]
    table = np.concatenate(columns, axis=1)
    high = table.astype(np.float32).astype(jnp.bfloat16)
    low = (table - high.astype(np.float64)).astype(np.float32).astype(jnp.bfloat16)
    return np.stack([high, low])


def split(x):
    high = x.astype(BF16)
    low = (x - high.astype(F32)).astype(BF16)
    return high, low


def dot3(x, table_ref, first, count, transposed):
    dims = (((1,), (1,)), ((), ())) if transposed else (((1,), (0,)), ((), ()))
    x_high, x_low = split(x)
    t_high = table_ref[0, :, first : first + count]
    t_low = table_ref[1, :, first : first + count]
    dot = functools.partial(lax.dot_general, dimension_numbers=dims, preferred_element_type=F32)
    return dot(x_high, t_high) + (dot(x_low, t_high) + dot(x_high, t_low))


def spin(x, shift):
    shift = shift % 128
    return x if shift == 0 else pltpu.roll(x, shift, axis=1)


def filter_rows(x, table_ref, limit):
    vec = x[0].shape[0]
    c1, c2 = math.cos(2 * math.pi / 5), math.cos(4 * math.pi / 5)
    s1, s2 = math.sin(2 * math.pi / 5), math.sin(4 * math.pi / 5)
    sum1, dif1 = x[1] + x[4], x[1] - x[4]
    sum2, dif2 = x[2] + x[3], x[2] - x[3]
    z0 = x[0] + sum1 + sum2
    z1 = jnp.concatenate([x[0] + c1 * sum1 + c2 * sum2, s1 * dif1 + s2 * dif2], axis=0)
    z2 = jnp.concatenate([x[0] + c2 * sum1 + c1 * sum2, s2 * dif1 - s1 * dif2], axis=0)
    lane = lax.broadcasted_iota(jnp.int32, (vec, 128), 1)
    half = lane < 64
    slot = jnp.where(half, lane, lane - 64)
    sign = jnp.where(half, 1.0, -1.0).astype(F32)

    wave0 = 5 * slot
    weight0 = jnp.where(wave0 <= limit, jnp.where(wave0 == 0, 1.0 / LON, 2.0 / LON), 0.0)
    spec0 = dot3(z0, table_ref, 0, 128, False) * weight0
    back0 = dot3(spec0, table_ref, 0, 128, True)
    backs = []
    for z, first, low_wave, high_wave in ((z1, 128, 1, 4), (z2, 384, 2, 3)):
        wave = 5 * slot + jnp.where(half, low_wave, high_wave)
        weight = jnp.where(wave <= limit, 2.0 / LON, 0.0)
        flip = weight * sign
        y = dot3(z, table_ref, first, 256, False)
        cc, cs = y[:vec, :128], y[:vec, 128:]
        sc, ss = y[vec:, :128], y[vec:, 128:]
        a = cc - sign * ss
        b = cs + sign * sc
        even = jnp.concatenate([a * weight, b * weight], axis=1)
        odd = jnp.concatenate([b * flip, -(a * flip)], axis=1)
        back = dot3(jnp.concatenate([even, odd], axis=0), table_ref, first, 256, True)
        backs += [back[:vec], back[vec:]]
    e1, o1, e2, o2 = backs
    out = [back0 + e1 + e2]
    p, m = back0 + c1 * e1 + c2 * e2, s1 * o1 + s2 * o2
    r, n = back0 + c2 * e1 + c1 * e2, s2 * o1 - s1 * o2
    return out + [p + m, r + n, r - n, p - m]


def wrapped(last, first, lane):
    return jnp.where(lane < 64, last, jnp.where(lane < 96, spin(first, 64), spin(last, 64)))


def iotas():
    return (
        lax.broadcasted_iota(jnp.int32, (8, 128), 1),
        lax.broadcasted_iota(jnp.int32, (8, 128), 0),
    )


def load_kernel(
    band_ref, u_hbm, v_hbm, h_hbm, t_hbm, table_hbm, cutoff_hbm,
    u_ref, v_ref, h_ref, t_ref, last_ref, first_ref, table_ref, cutoff_ref, sems,
):
    pairs = (
        (u_hbm, u_ref), (v_hbm, v_ref), (cutoff_hbm, cutoff_ref), (table_hbm, table_ref),
        (h_hbm, h_ref), (t_hbm, t_ref),
    )
    copies = [pltpu.make_async_copy(src, dst, sems.at[n]) for n, (src, dst) in enumerate(pairs)]
    for copy in copies:
        copy.start()
    band = band_ref[0]
    bands = POLAR // ROWS
    own = jnp.logical_or(band < bands, band >= BANDS - bands)
    entry = jnp.where(band < bands, band, band - (BANDS - 2 * bands)) * ROWS
    for copy in copies[:4]:
        copy.wait()

    @pl.when(own)
    def _():
        row = lax.broadcasted_iota(jnp.int32, (8, 128), 0)
        limit = jnp.zeros((8, 128), jnp.int32)
        for r in range(ROWS):
            limit = jnp.where(row == r, cutoff_ref[entry + r], limit)
        spans = [slice(PART * q, PART * (q + 1)) for q in range(RADIX)]
        x = [
            jnp.concatenate([ref[:, :, at].reshape(32, PART) for ref in (u_ref, v_ref)], axis=0)
            for at in spans
        ]
        for at, piece in zip(spans, filter_rows(x, table_ref, jnp.concatenate([limit] * 8, axis=0))):
            u_ref[:, :, at] = piece[0:32].reshape(4, 8, PART)
            v_ref[:, :, at] = piece[32:64].reshape(4, 8, PART)

    for f, ref in enumerate((v_ref, h_ref, t_ref)):
        if f:
            copies[f + 3].wait()
        for l in range(LEV_DEV):
            last_ref[f, l : l + 1, :] = ref[l, ROWS - 1 : ROWS, :]
            first_ref[f, l : l + 1, :] = ref[l, 0:1, :]


def place(slot_ref, fetch, lane, with_sides):
    for j in range(PEERS):
        tails = []
        for l in range(2):
            start = PIECE * j
            i, off = start // 128, start % 128
            slab = spin(fetch(l, i), -off)
            if off:
                slab = jnp.where(lane < 128 - off, slab, spin(fetch(l, i + 1), -off))
            slot_ref[j, l] = slab
            i, off = (start + 128) // 128, (start + 128) % 128
            tail = spin(fetch(l, i), 64 * l - off)
            if off > 64:
                other = spin(fetch(l, i + 1), 64 * l - off)
                tail = jnp.where(lane < 64 * l + 128 - off, tail, other)
            tails.append(tail)
        packed = jnp.where(lane < 64, tails[0], tails[1])
        if with_sides:
            at = (PIECE * j - 1) % LON
            i, off = at // 128, at % 128
            packed = jnp.where(
                lane == 127,
                spin(fetch(0, i), 127 - off),
                jnp.where(lane == 63, spin(fetch(1, i), 63 - off), packed),
            )
        slot_ref[j, 2] = packed


def send(slots_ref, out_hbm, sems, slot, group):
    dst = out_hbm.at[:, pl.ds(group, 3)]
    return pltpu.make_async_copy(slots_ref.at[slot], dst, sems.at[slot])


def advance_kernel(u_ref, v_ref, h_ref, t_ref, part_ref, out_hbm, tail_ref, slots_ref, sems):
    lane, row = iotas()
    fields = (u_ref, v_ref, h_ref, t_ref)
    for l in range(LEV_DEV):
        for f, ref in enumerate(fields):
            tail_ref[f, l, :, 0:64] = ref[l, :, LON - 64 : LON]
            tail_ref[f, l] = wrapped(tail_ref[f, l], ref[l, :, 0:128], lane)

    def put(pair, _):
        def fetch(l, i):
            if i == CHUNKS - 1:
                return tail_ref[0, 2 * pair + l]
            return u_ref[2 * pair + l, :, 128 * i : 128 * (i + 1)]

        place(slots_ref.at[pair], fetch, lane, False)
        send(slots_ref, out_hbm, sems, pair, 3 * pair).start()
        return 0

    lax.fori_loop(0, 2, put, 0)

    scale = COURANT * 0.25
    def level(l, _):

        def load(f, i):
            at = slice(128 * i, 128 * (i + 1))
            if i == CHUNKS - 1:
                return tail_ref[f, l]
            return fields[f][l, :, at]

        i = CHUNKS - 1
        u, h = load(0, i), load(2, i)
        q = h * load(3, i)
        before = tuple(spin(z, 1) for z in (u, h, q))
        flux = {}
        state = {}
        for i in range(CHUNKS + 1):
            if i < CHUNKS:
                u, v, h = load(0, i), load(1, i), load(2, i)
                q = h * load(3, i)
                now = tuple(spin(z, 1) for z in (u, h, q))
                ul, hl, ql = (jnp.where(lane == 0, b, n) for b, n in zip(before, now))
                before = now
                face = u + ul
                fh, fq = face * (h + hl), face * (q + ql)
                turned = (spin(fh, -1), spin(fq, -1))
                if i == 0:
                    first = turned
                vp, hp, qp = (pltpu.roll(z, 7, axis=0) for z in (v, h, q))
                wp = v + vp
                gh = jnp.where(row == 7, 0.0, wp * (h + hp))
                gq = jnp.where(row == 7, 0.0, wp * (q + qp))
                gh = gh - pltpu.roll(gh, 1, axis=0) - fh
                gq = gq - pltpu.roll(gq, 1, axis=0) - fq
                state[i] = (h, q, gh, gq)
                flux[i] = turned
            if i >= 1:
                k = i - 1
                nxt = flux[i] if i < CHUNKS else first
                h0, q0, gh0, gq0 = state.pop(k)
                mine = flux.pop(k)
                rh = jnp.where(lane == 127, nxt[0], mine[0])
                rq = jnp.where(lane == 127, nxt[1], mine[1])
                at = slice(128 * k, 128 * (k + 1))
                part_ref[0, l, :, at] = h0 - scale * (rh + gh0)
                part_ref[1, l, :, at] = q0 - scale * (rq + gq0)
        return 0

    lax.fori_loop(0, LEV_DEV, level, 0)
    for pair in range(2):
        send(slots_ref, out_hbm, sems, pair, 3 * pair).wait()


def pack_kernel(
    south_ref, north_ref, first_ref, last_ref, part_ref, wind_hbm,
    out_hbm, halo_ref, edge_ref, flux_ref, n_ref, slots_ref, sems,
):
    lane, row = iotas()
    end = slice(EXT - 128, EXT)
    for f in range(3):
        halo_ref[f, 0:4, 0:LON] = south_ref[f]
        halo_ref[f, 4:8, 0:LON] = north_ref[f]
        edge_ref[f, 0:4, 0:LON] = first_ref[f]
        edge_ref[f, 4:8, 0:LON] = last_ref[f]
        for ref in (halo_ref, edge_ref):
            ref[f, :, end] = wrapped(ref[f, :, end], ref[f, :, 0:128], lane)

    scale = COURANT * 0.25
    sign = jnp.where(row < 4, scale, -scale).astype(F32)
    for i in range(CHUNKS):
        at = slice(128 * i, 128 * (i + 1))
        v, h, t = (halo_ref[f, :, at] for f in range(3))
        w = (v + edge_ref[0, :, at]) * sign
        faces = w * (h + edge_ref[1, :, at]), w * (h * t + edge_ref[1, :, at] * edge_ref[2, :, at])
        for m, face in enumerate(faces):
            for r in range(8):
                flux_ref[m, r, :, at] = face[r : r + 1]

    def finish(l, _):
        for i in range(CHUNKS):
            at = slice(128 * i, 128 * (i + 1))

            def outer(m):
                low = jnp.broadcast_to(flux_ref[m, l, :, at], (8, 128))
                high = jnp.broadcast_to(flux_ref[m, l + 4, :, at], (8, 128))
                return jnp.where(row == 0, low, jnp.where(row == 7, high, 0.0))

            new_h = part_ref[0, l, :, at] + outer(0)
            new_q = part_ref[1, l, :, at] + outer(1)
            n_ref[0, l, :, at] = new_q / new_h
            n_ref[1, l, :, at] = new_h
        return 0

    lax.fori_loop(0, LEV_DEV, finish, 0)

    def put(pair, f):
        def fetch(l, i):
            return n_ref[f - 1, 2 * pair + l, :, 128 * i : 128 * (i + 1)]

        slot = 2 * (f - 1) + pair
        place(slots_ref.at[slot], fetch, lane, f == 2)
        send(slots_ref, out_hbm, sems, slot, 6 * f + 3 * pair).start()
        return 0

    for f in (1, 2):
        lax.fori_loop(0, 2, lambda pair, _, f=f: put(pair, f), 0)
    for f in (1, 2):
        for pair in range(2):
            send(slots_ref, out_hbm, sems, 2 * (f - 1) + pair, 6 * f + 3 * pair).wait()


EDGE, AU, BU, CU, FU, AT, BT, CT, FT = range(9)
BLOCK = 16
WINDOW = 11
UNROLL = 2
MARGIN = 1e-5


def remap_kernel(
    sigma_ref, inverse_ref, row_ref, r_ref, wind_hbm, temp_hbm,
    s_ref, d_ref, f_ref, m_ref, x_ref, y_ref, bound_ref, scalar_ref, wind_ref, temp_ref, sems, bound_sem,
):
    lane, row = iotas()
    left = lane < 64
    even = jnp.logical_or(jnp.logical_and(left, lane != 63), lane == 127)
    zero = jnp.zeros((8, 128), F32)

    def turn(x):
        return pltpu.roll(x, 64, axis=1)

    def unpack(n, carry):
        ea, eb, fua, fub, fta, ftb = carry
        for s in range(2):
            for pair in range(2):
                packs = [r_ref[2 * n + s, 6 * f + 3 * pair + 2] for f in range(3)]
                turns = [turn(p) for p in packs]
                for odd in range(2):
                    l = 2 * pair + odd
                    k = n * 8 + s * 4 + l
                    ua, ta, ha = (r_ref[2 * n + s, 6 * f + 3 * pair + odd] for f in range(3))
                    ub = turns[0] if odd else packs[0]
                    tb, hb = (
                        jnp.where(even, o, p) if odd else jnp.where(even, p, o)
                        for p, o in zip(packs[1:], turns[1:])
                    )
                    pa = ea + 0.5 * ha
                    pb = eb + 0.5 * hb
                    ra, rb = pltpu.roll(pa, 1, axis=1), pltpu.roll(pb, 1, axis=1)
                    la, lb = pltpu.roll(pa, 127, axis=1), pltpu.roll(pb, 127, axis=1)
                    wa = jnp.where(lane == 127, lb, la) - jnp.where(lane == 0, rb, ra)
                    wb = lb - jnp.where(lane == 0, ra, rb)
                    ua = ua - PRESSURE_COEF * wa
                    ub = ub - PRESSURE_COEF * wb
                    ub = jnp.where(left, ub, turn(ub))
                    s_ref[k, 0, EDGE], s_ref[k, 1, EDGE] = ea, eb
                    d_ref[k, 0], d_ref[k, 1] = ha, hb
                    s_ref[k, 0, FU], s_ref[k, 1, FU] = fua, fub
                    s_ref[k, 0, FT], s_ref[k, 1, FT] = fta, ftb
                    f_ref[0, k, 0], f_ref[0, k, 1] = ua, ub
                    f_ref[1, k, 0], f_ref[1, k, 1] = ta, tb
                    ea, eb = ea + ha, eb + hb
                    fua, fub = fua + ha * ua, fub + hb * ub
                    fta, ftb = fta + ha * ta, ftb + hb * tb
        return ea, eb, fua, fub, fta, ftb

    sums = lax.fori_loop(0, PEERS // 2, unpack, (zero,) * 6, unroll=4)
    surface = sums[:2]
    inverse = tuple(1.0 / s for s in surface)
    for k in range(WINDOW):
        s_ref[LEVELS + k, :, EDGE] = jnp.full((2, 8, 128), 1e30, F32)

    targets = jnp.broadcast_to(row_ref[...], (8, 128))

    def tally(n, _):
        for j in range(8):
            xa, xb = (s_ref[n * 8 + j, part, EDGE] * inverse[part] for part in range(2))
            x_ref[0, 8 * j : 8 * j + 8, :] = jnp.maximum(xa, xb)
            x_ref[1, 8 * j : 8 * j + 8, :] = jnp.minimum(xa, xb)
        for side, best in ((0, jnp.maximum), (1, jnp.minimum)):
            ref = x_ref.at[side]
            rows = [ref[pl.ds(r, 8, stride=8), :] for r in range(8)]
            while len(rows) > 1:
                rows = [best(p, q) for p, q in zip(rows[::2], rows[1::2])]
            y_ref[side, n] = rows[0]
        return 0

    lax.fori_loop(0, LEVELS // 8, tally, 0, unroll=2)
    counts = []
    for side, reduce, shift in ((0, jnp.max, -MARGIN), (1, jnp.min, MARGIN)):
        ends = [reduce(y_ref[side, n], axis=1, keepdims=True) for n in range(LEVELS // 8)]
        counts.append(sum(jnp.where(e <= targets + shift, 1.0, 0.0) for e in ends))
    low, high = (jnp.sum(c, axis=0, keepdims=True) for c in counts)
    low = jnp.maximum(low - 1.0, 0.0)
    bound_ref[...] = jnp.where(row == 0, low, high).astype(jnp.int32)
    to_scalars = pltpu.make_async_copy(bound_ref, scalar_ref, bound_sem)
    to_scalars.start()

    def middle(m, k):
        return (7.0 / 12.0) * (f_ref[m, k - 1] + f_ref[m, k]) - (1.0 / 12.0) * (
            f_ref[m, k - 2] + f_ref[m, k + 1]
        )

    def layer(k, lower, upper):
        rd = 1.0 / d_ref[k]
        square = rd * rd
        for m, (pa, pb, pc) in enumerate(((AU, BU, CU), (AT, BT, CT))):
            a0, a1, f = lower[m], upper[m], f_ref[m, k]
            rise, rest = f - a0, a1 - f
            s_ref[k, :, pa] = a0
            s_ref[k, :, pb] = rd * (rise + (rise - rest))
            s_ref[k, :, pc] = square * (rest - rise)

    def layers(n, lower):
        for j in range(4):
            k = 1 + 4 * n + j
            upper = tuple(middle(m, k + 1) for m in range(2))
            layer(k, lower, upper)
            lower = upper
        return lower

    last = LEVELS - 1
    second = tuple(0.5 * (f_ref[m, 0] + f_ref[m, 1]) for m in range(2))
    layer(0, tuple(f_ref[m, 0] for m in range(2)), second)
    lower = lax.fori_loop(0, 15, layers, second)
    for k in range(61, LEVELS):
        if k < last - 1:
            upper = tuple(middle(m, k + 1) for m in range(2))
        elif k == last - 1:
            upper = tuple(0.5 * (f_ref[m, last - 1] + f_ref[m, last]) for m in range(2))
        else:
            upper = tuple(f_ref[m, last] for m in range(2))
        layer(k, lower, upper)
        lower = upper

    to_scalars.wait()

    def places(g):
        i = 2 * g
        s0, s1 = sigma_ref[i], sigma_ref[i + 1]
        return (
            (surface[0] * s0, 0),
            (surface[0] * s1, 0),
            (surface[1] * jnp.where(left, s0, s1), 1),
        )

    def begin(points, low):
        return tuple(tuple(s_ref[low, part, plane] for plane in range(9)) for _, part in points)

    def pick(points, k, state):
        values = [[s_ref[k, part, plane] for plane in range(9)] for part in range(2)]
        out = []
        for (p, part), held in zip(points, state):
            inside = p >= values[part][EDGE]
            out.append(tuple(jnp.where(inside, v, h) for v, h in zip(values[part], held)))
        return tuple(out)

    def mass_of(g, points, state):
        slots = (2 * g, 2 * g + 1, LEVELS + g)
        for slot, (p, _), held in zip(slots, points, state):
            y = p - held[EDGE]
            for m, (a, b, c, f) in enumerate(((AU, BU, CU, FU), (AT, BT, CT, FT))):
                m_ref[m, slot] = held[f] + y * (held[a] + y * (held[b] + y * held[c]))

    def pairs(n, _):
        for j in range(UNROLL):
            g = UNROLL * n + j
            points = places(g)
            low = scalar_ref[0, 2 * g]
            state = begin(points, low)
            for k in range(1, WINDOW):
                state = pick(points, low + k, state)
            mass_of(g, points, state)
        for j in range(UNROLL):
            g = UNROLL * n + j
            low, high = scalar_ref[0, 2 * g], scalar_ref[1, 2 * g + 1]

            @pl.when(high - low > WINDOW)
            def _():
                points = places(g)
                state = lax.fori_loop(
                    low + 1, high, functools.partial(pick, points), begin(points, low)
                )
                mass_of(g, points, state)

        return 0

    def leave(b, m):
        ref, hbm = ((wind_ref, wind_hbm), (temp_ref, temp_hbm))[m]
        at = pl.ds(b * BLOCK, BLOCK)
        return pltpu.make_async_copy(ref.at[at], hbm.at[at], sems.at[m, b])

    def block(b, carry):
        lax.fori_loop(b * (BLOCK // 2 // UNROLL), (b + 1) * (BLOCK // 2 // UNROLL), pairs, 0)
        carry = list(carry)
        for m, ref in enumerate((wind_ref, temp_ref)):
            for j in range(BLOCK // 2):
                i = b * BLOCK + 2 * j
                masses = m_ref[m, i], m_ref[m, i + 1]
                tail = m_ref[m, LEVELS + b * (BLOCK // 2) + j]
                turned = turn(tail)
                tails = tail, turned
                for n in range(2):
                    width = inverse_ref[i + n]
                    ref[i + n, :, 0:128] = (masses[n] - carry[2 * m]) * (inverse[0] * width)
                    value = (tails[n] - carry[2 * m + 1]) * (inverse[1] * width)
                    ref[i + n, :, 128:PIECE] = value[:, 0:TAIL]
                    carry[2 * m], carry[2 * m + 1] = masses[n], tails[n]
            leave(b, m).start()
        return tuple(carry)

    lax.fori_loop(0, LEVELS // BLOCK, block, (zero,) * 4)
    for b in range(LEVELS // BLOCK):
        for m in range(2):
            leave(b, m).wait()


VMEM = pltpu.MemorySpace.VMEM


def whole(space=pltpu.VMEM):
    return pl.BlockSpec(memory_space=space)


def keep(x):
    return pltpu.with_memory_space_constraint(x, VMEM)


def local(zonal_wind, merid_wind, thickness, potential_temp, cutoff, sigma_weights):
    band = lax.axis_index("lat").astype(jnp.int32).reshape(1)
    up = [(i, i + 1) for i in range(BANDS - 1)]
    down = [(i + 1, i) for i in range(BANDS - 1)]
    inputs = (zonal_wind, merid_wind, thickness, potential_temp)
    edge = pltpu.VMEM((3, LEV_DEV, LON), F32)
    field = pltpu.VMEM((LEV_DEV, ROWS, LON), F32)
    table = mode_table()
    *fields, last, first = pl.pallas_call(
        load_kernel,
        name="load",
        compiler_params=pltpu.CompilerParams(vmem_limit_bytes=16 << 20),
        out_shape=(field,) * 4 + (edge,) * 2,
        in_specs=[whole(pltpu.SMEM)] + [whole(pltpu.HBM)] * 6,
        out_specs=(whole(),) * 6,
        scratch_shapes=[
            pltpu.VMEM(table.shape, BF16),
            pltpu.SMEM(cutoff.shape, jnp.int32),
            pltpu.SemaphoreType.DMA((6,)),
        ],
    )(
        band,
        *(
            pltpu.with_memory_space_constraint(x, pltpu.HBM)
            for x in (*inputs, jnp.asarray(table), cutoff)
        ),
    )
    fields = [keep(x) for x in fields]
    south = lax.ppermute(last, "lat", up)
    north = lax.ppermute(first, "lat", down)
    window = jax.ShapeDtypeStruct((PEERS, 18, 8, 128), F32)
    slot = (PEERS, 3, 8, 128)
    part, winds = pl.pallas_call(
        advance_kernel,
        name="advance",
        compiler_params=pltpu.CompilerParams(vmem_limit_bytes=16 << 20),
        out_shape=(pltpu.VMEM((2, LEV_DEV, ROWS, EXT), F32), window),
        in_specs=[whole()] * 4,
        out_specs=(whole(), whole(pltpu.HBM)),
        scratch_shapes=[
            pltpu.VMEM((4, LEV_DEV, ROWS, 128), F32),
            pltpu.VMEM((2, *slot), F32),
            pltpu.SemaphoreType.DMA((2,)),
        ],
    )(*fields)
    outgoing = pl.pallas_call(
        pack_kernel,
        name="pack",
        compiler_params=pltpu.CompilerParams(vmem_limit_bytes=16 << 20),
        out_shape=window,
        input_output_aliases={5: 0},
        in_specs=[whole()] * 5 + [whole(pltpu.HBM)],
        out_specs=whole(pltpu.HBM),
        scratch_shapes=[
            pltpu.VMEM((3, 8, EXT), F32),
            pltpu.VMEM((3, 8, EXT), F32),
            pltpu.VMEM((2, 8, 1, EXT), F32),
            pltpu.VMEM((2, LEV_DEV, ROWS, EXT), F32),
            pltpu.VMEM((4, *slot), F32),
            pltpu.SemaphoreType.DMA((4,)),
        ],
    )(*map(keep, (south, north, first, last, part)), winds)
    columns = lax.all_to_all(outgoing, "lev", split_axis=0, concat_axis=0, tiled=True)
    total = jnp.sum(sigma_weights)
    sigma = jnp.cumsum(sigma_weights) / total
    inverse = total / sigma_weights
    sigma_row = jnp.pad(sigma, (0, 128 - LEVELS), constant_values=2.0).reshape(1, 128)
    shape = jax.ShapeDtypeStruct((LEVELS, ROWS, PIECE), F32)
    return pl.pallas_call(
        remap_kernel,
        name="remap",
        compiler_params=pltpu.CompilerParams(vmem_limit_bytes=24 << 20),
        out_shape=(shape, shape),
        in_specs=[whole(pltpu.SMEM)] * 2 + [whole()] * 2,
        out_specs=(whole(pltpu.HBM), whole(pltpu.HBM)),
        scratch_shapes=[
            pltpu.VMEM((LEVELS + WINDOW, 2, 9, 8, 128), F32),
            pltpu.VMEM((LEVELS, 2, 8, 128), F32),
            pltpu.VMEM((2, LEVELS, 2, 8, 128), F32),
            pltpu.VMEM((2, LEVELS + LEVELS // 2, 8, 128), F32),
            pltpu.VMEM((2, 64, 128), F32),
            pltpu.VMEM((2, LEVELS // 8, 8, 128), F32),
            pltpu.VMEM((8, 128), jnp.int32),
            pltpu.SMEM((8, 128), jnp.int32),
            pltpu.VMEM((LEVELS, ROWS, PIECE), F32),
            pltpu.VMEM((LEVELS, ROWS, PIECE), F32),
            pltpu.SemaphoreType.DMA((2, LEVELS // BLOCK)),
            pltpu.SemaphoreType.DMA,
        ],
    )(sigma, inverse, sigma_row, keep(columns))


def solution(mesh):
    field = P("lev", "lat", None)
    out = P(None, "lat", "lev")
    return jax.shard_map(
        local,
        mesh=mesh,
        in_specs=(field, field, field, field, P(), P()),
        out_specs=(out, out),
        check_vma=False,
    )
```

```python
import functools
import math

import jax
import jax.numpy as jnp
import numpy as np
from jax import lax
from jax.experimental import pallas as pl
from jax.experimental.pallas import tpu as pltpu
from jax.sharding import PartitionSpec as P

F32 = jnp.float32
BF16 = jnp.bfloat16

LON = 2880
EXT = 2944
CHUNKS = EXT // 128
LEVELS = 64
ROWS = 8
LEV_DEV = 4
BANDS = 32
PEERS = 16
PIECE = LON // PEERS
TAIL = PIECE - 128
RADIX = 5
PART = LON // RADIX
POLAR = 16
COURANT = 0.02
PRESSURE_COEF = 0.05


def mode_table():
    j = np.arange(64)
    orders = [[5 * j], [5 * j + 1, 5 * j + 4], [5 * j + 2, 5 * j + 3]]
    r = np.arange(PART)
    columns = []
    for order in orders:
        waves = np.concatenate(order)
        angle = 2.0 * np.pi * ((r[:, None] * waves[None, :]) % LON) / LON
        columns += [np.cos(angle), np.sin(angle)]
    table = np.concatenate(columns, axis=1)
    high = table.astype(np.float32).astype(jnp.bfloat16)
    low = (table - high.astype(np.float64)).astype(np.float32).astype(jnp.bfloat16)
    return np.stack([high, low])


def split(x):
    high = x.astype(BF16)
    low = (x - high.astype(F32)).astype(BF16)
    return high, low


def dot3(x, table_ref, first, count, transposed):
    dims = (((1,), (1,)), ((), ())) if transposed else (((1,), (0,)), ((), ()))
    x_high, x_low = split(x)
    t_high = table_ref[0, :, first : first + count]
    t_low = table_ref[1, :, first : first + count]
    dot = functools.partial(lax.dot_general, dimension_numbers=dims, preferred_element_type=F32)
    return dot(x_high, t_high) + (dot(x_low, t_high) + dot(x_high, t_low))


def spin(x, shift):
    shift = shift % 128
    return x if shift == 0 else pltpu.roll(x, shift, axis=1)


def filter_rows(x, table_ref, limit):
    vec = x[0].shape[0]
    c1, c2 = math.cos(2 * math.pi / 5), math.cos(4 * math.pi / 5)
    s1, s2 = math.sin(2 * math.pi / 5), math.sin(4 * math.pi / 5)
    sum1, dif1 = x[1] + x[4], x[1] - x[4]
    sum2, dif2 = x[2] + x[3], x[2] - x[3]
    z0 = x[0] + sum1 + sum2
    z1 = jnp.concatenate([x[0] + c1 * sum1 + c2 * sum2, s1 * dif1 + s2 * dif2], axis=0)
    z2 = jnp.concatenate([x[0] + c2 * sum1 + c1 * sum2, s2 * dif1 - s1 * dif2], axis=0)
    lane = lax.broadcasted_iota(jnp.int32, (vec, 128), 1)
    half = lane < 64
    slot = jnp.where(half, lane, lane - 64)
    sign = jnp.where(half, 1.0, -1.0).astype(F32)

    wave0 = 5 * slot
    weight0 = jnp.where(wave0 <= limit, jnp.where(wave0 == 0, 1.0 / LON, 2.0 / LON), 0.0)
    spec0 = dot3(z0, table_ref, 0, 128, False) * weight0
    back0 = dot3(spec0, table_ref, 0, 128, True)
    backs = []
    for z, first, low_wave, high_wave in ((z1, 128, 1, 4), (z2, 384, 2, 3)):
        wave = 5 * slot + jnp.where(half, low_wave, high_wave)
        weight = jnp.where(wave <= limit, 2.0 / LON, 0.0)
        flip = weight * sign
        y = dot3(z, table_ref, first, 256, False)
        cc, cs = y[:vec, :128], y[:vec, 128:]
        sc, ss = y[vec:, :128], y[vec:, 128:]
        a = cc - sign * ss
        b = cs + sign * sc
        even = jnp.concatenate([a * weight, b * weight], axis=1)
        odd = jnp.concatenate([b * flip, -(a * flip)], axis=1)
        back = dot3(jnp.concatenate([even, odd], axis=0), table_ref, first, 256, True)
        backs += [back[:vec], back[vec:]]
    e1, o1, e2, o2 = backs
    out = [back0 + e1 + e2]
    p, m = back0 + c1 * e1 + c2 * e2, s1 * o1 + s2 * o2
    r, n = back0 + c2 * e1 + c1 * e2, s2 * o1 - s1 * o2
    return out + [p + m, r + n, r - n, p - m]


def wrapped(last, first, lane):
    return jnp.where(lane < 64, last, jnp.where(lane < 96, spin(first, 64), spin(last, 64)))


def iotas():
    return (
        lax.broadcasted_iota(jnp.int32, (8, 128), 1),
        lax.broadcasted_iota(jnp.int32, (8, 128), 0),
    )


def load_kernel(
    band_ref, u_hbm, v_hbm, h_hbm, t_hbm, table_hbm, cutoff_hbm,
    u_ref, v_ref, h_ref, t_ref, last_ref, first_ref, table_ref, cutoff_ref, sems,
):
    pairs = (
        (u_hbm, u_ref), (v_hbm, v_ref), (cutoff_hbm, cutoff_ref), (table_hbm, table_ref),
        (h_hbm, h_ref), (t_hbm, t_ref),
    )
    copies = [pltpu.make_async_copy(src, dst, sems.at[n]) for n, (src, dst) in enumerate(pairs)]
    for copy in copies:
        copy.start()
    band = band_ref[0]
    bands = POLAR // ROWS
    own = jnp.logical_or(band < bands, band >= BANDS - bands)
    entry = jnp.where(band < bands, band, band - (BANDS - 2 * bands)) * ROWS
    for copy in copies[:4]:
        copy.wait()

    @pl.when(own)
    def _():
        row = lax.broadcasted_iota(jnp.int32, (8, 128), 0)
        limit = jnp.zeros((8, 128), jnp.int32)
        for r in range(ROWS):
            limit = jnp.where(row == r, cutoff_ref[entry + r], limit)
        spans = [slice(PART * q, PART * (q + 1)) for q in range(RADIX)]
        x = [
            jnp.concatenate([ref[:, :, at].reshape(32, PART) for ref in (u_ref, v_ref)], axis=0)
            for at in spans
        ]
        for at, piece in zip(spans, filter_rows(x, table_ref, jnp.concatenate([limit] * 8, axis=0))):
            u_ref[:, :, at] = piece[0:32].reshape(4, 8, PART)
            v_ref[:, :, at] = piece[32:64].reshape(4, 8, PART)

    for f, ref in enumerate((v_ref, h_ref, t_ref)):
        if f:
            copies[f + 3].wait()
        for l in range(LEV_DEV):
            last_ref[f, l : l + 1, :] = ref[l, ROWS - 1 : ROWS, :]
            first_ref[f, l : l + 1, :] = ref[l, 0:1, :]


def place(slot_ref, fetch, lane, with_sides):
    for j in range(PEERS):
        tails = []
        for l in range(2):
            start = PIECE * j
            i, off = start // 128, start % 128
            slab = spin(fetch(l, i), -off)
            if off:
                slab = jnp.where(lane < 128 - off, slab, spin(fetch(l, i + 1), -off))
            slot_ref[j, l] = slab
            i, off = (start + 128) // 128, (start + 128) % 128
            tail = spin(fetch(l, i), 64 * l - off)
            if off > 64:
                other = spin(fetch(l, i + 1), 64 * l - off)
                tail = jnp.where(lane < 64 * l + 128 - off, tail, other)
            tails.append(tail)
        packed = jnp.where(lane < 64, tails[0], tails[1])
        if with_sides:
            at = (PIECE * j - 1) % LON
            i, off = at // 128, at % 128
            packed = jnp.where(
                lane == 127,
                spin(fetch(0, i), 127 - off),
                jnp.where(lane == 63, spin(fetch(1, i), 63 - off), packed),
            )
        slot_ref[j, 2] = packed


def send(slots_ref, out_hbm, sems, slot, group):
    dst = out_hbm.at[:, pl.ds(group, 3)]
    return pltpu.make_async_copy(slots_ref.at[slot], dst, sems.at[slot])


def advance_kernel(u_ref, v_ref, h_ref, t_ref, part_ref, out_hbm, tail_ref, slots_ref, sems):
    lane, row = iotas()
    fields = (u_ref, v_ref, h_ref, t_ref)
    for l in range(LEV_DEV):
        for f, ref in enumerate(fields):
            tail_ref[f, l, :, 0:64] = ref[l, :, LON - 64 : LON]
            tail_ref[f, l] = wrapped(tail_ref[f, l], ref[l, :, 0:128], lane)

    def put(pair, _):
        def fetch(l, i):
            if i == CHUNKS - 1:
                return tail_ref[0, 2 * pair + l]
            return u_ref[2 * pair + l, :, 128 * i : 128 * (i + 1)]

        place(slots_ref.at[pair], fetch, lane, False)
        send(slots_ref, out_hbm, sems, pair, 3 * pair).start()
        return 0

    lax.fori_loop(0, 2, put, 0)

    scale = COURANT * 0.25
    def level(l, _):

        def load(f, i):
            at = slice(128 * i, 128 * (i + 1))
            if i == CHUNKS - 1:
                return tail_ref[f, l]
            return fields[f][l, :, at]

        i = CHUNKS - 1
        u, h = load(0, i), load(2, i)
        q = h * load(3, i)
        before = tuple(spin(z, 1) for z in (u, h, q))
        flux = {}
        state = {}
        for i in range(CHUNKS + 1):
            if i < CHUNKS:
                u, v, h = load(0, i), load(1, i), load(2, i)
                q = h * load(3, i)
                now = tuple(spin(z, 1) for z in (u, h, q))
                ul, hl, ql = (jnp.where(lane == 0, b, n) for b, n in zip(before, now))
                before = now
                face = u + ul
                fh, fq = face * (h + hl), face * (q + ql)
                turned = (spin(fh, -1), spin(fq, -1))
                if i == 0:
                    first = turned
                vp, hp, qp = (pltpu.roll(z, 7, axis=0) for z in (v, h, q))
                wp = v + vp
                gh = jnp.where(row == 7, 0.0, wp * (h + hp))
                gq = jnp.where(row == 7, 0.0, wp * (q + qp))
                gh = gh - pltpu.roll(gh, 1, axis=0) - fh
                gq = gq - pltpu.roll(gq, 1, axis=0) - fq
                state[i] = (h, q, gh, gq)
                flux[i] = turned
            if i >= 1:
                k = i - 1
                nxt = flux[i] if i < CHUNKS else first
                h0, q0, gh0, gq0 = state.pop(k)
                mine = flux.pop(k)
                rh = jnp.where(lane == 127, nxt[0], mine[0])
                rq = jnp.where(lane == 127, nxt[1], mine[1])
                at = slice(128 * k, 128 * (k + 1))
                part_ref[0, l, :, at] = h0 - scale * (rh + gh0)
                part_ref[1, l, :, at] = q0 - scale * (rq + gq0)
        return 0

    lax.fori_loop(0, LEV_DEV, level, 0)
    for pair in range(2):
        send(slots_ref, out_hbm, sems, pair, 3 * pair).wait()


def pack_kernel(
    south_ref, north_ref, first_ref, last_ref, part_ref, wind_hbm,
    out_hbm, halo_ref, edge_ref, flux_ref, n_ref, slots_ref, sems,
):
    lane, row = iotas()
    end = slice(EXT - 128, EXT)
    for f in range(3):
        halo_ref[f, 0:4, 0:LON] = south_ref[f]
        halo_ref[f, 4:8, 0:LON] = north_ref[f]
        edge_ref[f, 0:4, 0:LON] = first_ref[f]
        edge_ref[f, 4:8, 0:LON] = last_ref[f]
        for ref in (halo_ref, edge_ref):
            ref[f, :, end] = wrapped(ref[f, :, end], ref[f, :, 0:128], lane)

    scale = COURANT * 0.25
    sign = jnp.where(row < 4, scale, -scale).astype(F32)
    for i in range(CHUNKS):
        at = slice(128 * i, 128 * (i + 1))
        v, h, t = (halo_ref[f, :, at] for f in range(3))
        w = (v + edge_ref[0, :, at]) * sign
        faces = w * (h + edge_ref[1, :, at]), w * (h * t + edge_ref[1, :, at] * edge_ref[2, :, at])
        for m, face in enumerate(faces):
            for r in range(8):
                flux_ref[m, r, :, at] = face[r : r + 1]

    def finish(l, _):
        for i in range(CHUNKS):
            at = slice(128 * i, 128 * (i + 1))

            def outer(m):
                low = jnp.broadcast_to(flux_ref[m, l, :, at], (8, 128))
                high = jnp.broadcast_to(flux_ref[m, l + 4, :, at], (8, 128))
                return jnp.where(row == 0, low, jnp.where(row == 7, high, 0.0))

            new_h = part_ref[0, l, :, at] + outer(0)
            new_q = part_ref[1, l, :, at] + outer(1)
            n_ref[0, l, :, at] = new_q / new_h
            n_ref[1, l, :, at] = new_h
        return 0

    lax.fori_loop(0, LEV_DEV, finish, 0, unroll=2)

    def put(pair, f):
        def fetch(l, i):
            return n_ref[f - 1, 2 * pair + l, :, 128 * i : 128 * (i + 1)]

        slot = 2 * (f - 1) + pair
        place(slots_ref.at[slot], fetch, lane, f == 2)
        send(slots_ref, out_hbm, sems, slot, 6 * f + 3 * pair).start()
        return 0

    for f in (1, 2):
        lax.fori_loop(0, 2, lambda pair, _, f=f: put(pair, f), 0)
    for f in (1, 2):
        for pair in range(2):
            send(slots_ref, out_hbm, sems, 2 * (f - 1) + pair, 6 * f + 3 * pair).wait()


EDGE, AU, BU, CU, FU, AT, BT, CT, FT = range(9)
BLOCK = 16
WINDOW = 11
UNROLL = 2
MARGIN = 1e-5


def remap_kernel(
    sigma_ref, inverse_ref, row_ref, r_ref, wind_hbm, temp_hbm,
    s_ref, d_ref, f_ref, m_ref, x_ref, y_ref, bound_ref, scalar_ref, wind_ref, temp_ref, sems, bound_sem,
):
    lane, row = iotas()
    left = lane < 64
    even = jnp.logical_or(jnp.logical_and(left, lane != 63), lane == 127)
    zero = jnp.zeros((8, 128), F32)

    def turn(x):
        return pltpu.roll(x, 64, axis=1)

    def unpack(n, carry):
        ea, eb, fua, fub, fta, ftb = carry
        for s in range(2):
            for pair in range(2):
                packs = [r_ref[2 * n + s, 6 * f + 3 * pair + 2] for f in range(3)]
                turns = [turn(p) for p in packs]
                for odd in range(2):
                    l = 2 * pair + odd
                    k = n * 8 + s * 4 + l
                    ua, ta, ha = (r_ref[2 * n + s, 6 * f + 3 * pair + odd] for f in range(3))
                    ub = turns[0] if odd else packs[0]
                    tb, hb = (
                        jnp.where(even, o, p) if odd else jnp.where(even, p, o)
                        for p, o in zip(packs[1:], turns[1:])
                    )
                    pa = ea + 0.5 * ha
                    pb = eb + 0.5 * hb
                    ra, rb = pltpu.roll(pa, 1, axis=1), pltpu.roll(pb, 1, axis=1)
                    la, lb = pltpu.roll(pa, 127, axis=1), pltpu.roll(pb, 127, axis=1)
                    wa = jnp.where(lane == 127, lb, la) - jnp.where(lane == 0, rb, ra)
                    wb = lb - jnp.where(lane == 0, ra, rb)
                    ua = ua - PRESSURE_COEF * wa
                    ub = ub - PRESSURE_COEF * wb
                    ub = jnp.where(left, ub, turn(ub))
                    s_ref[k, 0, EDGE], s_ref[k, 1, EDGE] = ea, eb
                    d_ref[k, 0], d_ref[k, 1] = ha, hb
                    s_ref[k, 0, FU], s_ref[k, 1, FU] = fua, fub
                    s_ref[k, 0, FT], s_ref[k, 1, FT] = fta, ftb
                    f_ref[0, k, 0], f_ref[0, k, 1] = ua, ub
                    f_ref[1, k, 0], f_ref[1, k, 1] = ta, tb
                    ea, eb = ea + ha, eb + hb
                    fua, fub = fua + ha * ua, fub + hb * ub
                    fta, ftb = fta + ha * ta, ftb + hb * tb
        return ea, eb, fua, fub, fta, ftb

    sums = lax.fori_loop(0, PEERS // 2, unpack, (zero,) * 6, unroll=4)
    surface = sums[:2]
    inverse = tuple(1.0 / s for s in surface)
    for k in range(WINDOW):
        s_ref[LEVELS + k, :, EDGE] = jnp.full((2, 8, 128), 1e30, F32)

    targets = jnp.broadcast_to(row_ref[...], (8, 128))

    def tally(n, _):
        for j in range(8):
            xa, xb = (s_ref[n * 8 + j, part, EDGE] * inverse[part] for part in range(2))
            x_ref[0, 8 * j : 8 * j + 8, :] = jnp.maximum(xa, xb)
            x_ref[1, 8 * j : 8 * j + 8, :] = jnp.minimum(xa, xb)
        for side, best in ((0, jnp.maximum), (1, jnp.minimum)):
            ref = x_ref.at[side]
            rows = [ref[pl.ds(r, 8, stride=8), :] for r in range(8)]
            while len(rows) > 1:
                rows = [best(p, q) for p, q in zip(rows[::2], rows[1::2])]
            y_ref[side, n] = rows[0]
        return 0

    lax.fori_loop(0, LEVELS // 8, tally, 0, unroll=2)
    counts = []
    for side, reduce, shift in ((0, jnp.max, -MARGIN), (1, jnp.min, MARGIN)):
        ends = [reduce(y_ref[side, n], axis=1, keepdims=True) for n in range(LEVELS // 8)]
        counts.append(sum(jnp.where(e <= targets + shift, 1.0, 0.0) for e in ends))
    low, high = (jnp.sum(c, axis=0, keepdims=True) for c in counts)
    low = jnp.maximum(low - 1.0, 0.0)
    bound_ref[...] = jnp.where(row == 0, low, high).astype(jnp.int32)
    to_scalars = pltpu.make_async_copy(bound_ref, scalar_ref, bound_sem)
    to_scalars.start()

    def middle(m, k):
        return (7.0 / 12.0) * (f_ref[m, k - 1] + f_ref[m, k]) - (1.0 / 12.0) * (
            f_ref[m, k - 2] + f_ref[m, k + 1]
        )

    def layer(k, lower, upper):
        rd = 1.0 / d_ref[k]
        square = rd * rd
        for m, (pa, pb, pc) in enumerate(((AU, BU, CU), (AT, BT, CT))):
            a0, a1, f = lower[m], upper[m], f_ref[m, k]
            rise, rest = f - a0, a1 - f
            s_ref[k, :, pa] = a0
            s_ref[k, :, pb] = rd * (rise + (rise - rest))
            s_ref[k, :, pc] = square * (rest - rise)

    def layers(n, lower):
        for j in range(4):
            k = 1 + 4 * n + j
            upper = tuple(middle(m, k + 1) for m in range(2))
            layer(k, lower, upper)
            lower = upper
        return lower

    last = LEVELS - 1
    second = tuple(0.5 * (f_ref[m, 0] + f_ref[m, 1]) for m in range(2))
    layer(0, tuple(f_ref[m, 0] for m in range(2)), second)
    lower = lax.fori_loop(0, 15, layers, second)
    for k in range(61, LEVELS):
        if k < last - 1:
            upper = tuple(middle(m, k + 1) for m in range(2))
        elif k == last - 1:
            upper = tuple(0.5 * (f_ref[m, last - 1] + f_ref[m, last]) for m in range(2))
        else:
            upper = tuple(f_ref[m, last] for m in range(2))
        layer(k, lower, upper)
        lower = upper

    to_scalars.wait()

    def places(g):
        i = 2 * g
        s0, s1 = sigma_ref[i], sigma_ref[i + 1]
        return (
            (surface[0] * s0, 0),
            (surface[0] * s1, 0),
            (surface[1] * jnp.where(left, s0, s1), 1),
        )

    def begin(points, low):
        return tuple(tuple(s_ref[low, part, plane] for plane in range(9)) for _, part in points)

    def pick(points, k, state):
        values = [[s_ref[k, part, plane] for plane in range(9)] for part in range(2)]
        out = []
        for (p, part), held in zip(points, state):
            inside = p >= values[part][EDGE]
            out.append(tuple(jnp.where(inside, v, h) for v, h in zip(values[part], held)))
        return tuple(out)

    def mass_of(g, points, state):
        slots = (2 * g, 2 * g + 1, LEVELS + g)
        for slot, (p, _), held in zip(slots, points, state):
            y = p - held[EDGE]
            for m, (a, b, c, f) in enumerate(((AU, BU, CU, FU), (AT, BT, CT, FT))):
                m_ref[m, slot] = held[f] + y * (held[a] + y * (held[b] + y * held[c]))

    def pairs(n, _):
        for j in range(UNROLL):
            g = UNROLL * n + j
            points = places(g)
            low = scalar_ref[0, 2 * g]
            state = begin(points, low)
            for k in range(1, WINDOW):
                state = pick(points, low + k, state)
            mass_of(g, points, state)
        for j in range(UNROLL):
            g = UNROLL * n + j
            low, high = scalar_ref[0, 2 * g], scalar_ref[1, 2 * g + 1]

            @pl.when(high - low > WINDOW)
            def _():
                points = places(g)
                state = lax.fori_loop(
                    low + 1, high, functools.partial(pick, points), begin(points, low)
                )
                mass_of(g, points, state)

        return 0

    def leave(b, m):
        ref, hbm = ((wind_ref, wind_hbm), (temp_ref, temp_hbm))[m]
        at = pl.ds(b * BLOCK, BLOCK)
        return pltpu.make_async_copy(ref.at[at], hbm.at[at], sems.at[m, b])

    def block(b, carry):
        lax.fori_loop(b * (BLOCK // 2 // UNROLL), (b + 1) * (BLOCK // 2 // UNROLL), pairs, 0)
        carry = list(carry)
        for m, ref in enumerate((wind_ref, temp_ref)):
            for j in range(BLOCK // 2):
                i = b * BLOCK + 2 * j
                masses = m_ref[m, i], m_ref[m, i + 1]
                tail = m_ref[m, LEVELS + b * (BLOCK // 2) + j]
                turned = turn(tail)
                tails = tail, turned
                for n in range(2):
                    width = inverse_ref[i + n]
                    ref[i + n, :, 0:128] = (masses[n] - carry[2 * m]) * (inverse[0] * width)
                    value = (tails[n] - carry[2 * m + 1]) * (inverse[1] * width)
                    ref[i + n, :, 128:PIECE] = value[:, 0:TAIL]
                    carry[2 * m], carry[2 * m + 1] = masses[n], tails[n]
            leave(b, m).start()
        return tuple(carry)

    lax.fori_loop(0, LEVELS // BLOCK, block, (zero,) * 4)
    for b in range(LEVELS // BLOCK):
        for m in range(2):
            leave(b, m).wait()


VMEM = pltpu.MemorySpace.VMEM


def whole(space=pltpu.VMEM):
    return pl.BlockSpec(memory_space=space)


def keep(x):
    return pltpu.with_memory_space_constraint(x, VMEM)


def local(zonal_wind, merid_wind, thickness, potential_temp, cutoff, sigma_weights):
    band = lax.axis_index("lat").astype(jnp.int32).reshape(1)
    up = [(i, i + 1) for i in range(BANDS - 1)]
    down = [(i + 1, i) for i in range(BANDS - 1)]
    inputs = (zonal_wind, merid_wind, thickness, potential_temp)
    edge = pltpu.VMEM((3, LEV_DEV, LON), F32)
    field = pltpu.VMEM((LEV_DEV, ROWS, LON), F32)
    table = mode_table()
    *fields, last, first = pl.pallas_call(
        load_kernel,
        name="load",
        compiler_params=pltpu.CompilerParams(vmem_limit_bytes=16 << 20),
        out_shape=(field,) * 4 + (edge,) * 2,
        in_specs=[whole(pltpu.SMEM)] + [whole(pltpu.HBM)] * 6,
        out_specs=(whole(),) * 6,
        scratch_shapes=[
            pltpu.VMEM(table.shape, BF16),
            pltpu.SMEM(cutoff.shape, jnp.int32),
            pltpu.SemaphoreType.DMA((6,)),
        ],
    )(
        band,
        *(
            pltpu.with_memory_space_constraint(x, pltpu.HBM)
            for x in (*inputs, jnp.asarray(table), cutoff)
        ),
    )
    fields = [keep(x) for x in fields]
    south = lax.ppermute(last, "lat", up)
    north = lax.ppermute(first, "lat", down)
    window = jax.ShapeDtypeStruct((PEERS, 18, 8, 128), F32)
    slot = (PEERS, 3, 8, 128)
    part, winds = pl.pallas_call(
        advance_kernel,
        name="advance",
        compiler_params=pltpu.CompilerParams(vmem_limit_bytes=16 << 20),
        out_shape=(pltpu.VMEM((2, LEV_DEV, ROWS, EXT), F32), window),
        in_specs=[whole()] * 4,
        out_specs=(whole(), whole(pltpu.HBM)),
        scratch_shapes=[
            pltpu.VMEM((4, LEV_DEV, ROWS, 128), F32),
            pltpu.VMEM((2, *slot), F32),
            pltpu.SemaphoreType.DMA((2,)),
        ],
    )(*fields)
    outgoing = pl.pallas_call(
        pack_kernel,
        name="pack",
        compiler_params=pltpu.CompilerParams(vmem_limit_bytes=16 << 20),
        out_shape=window,
        input_output_aliases={5: 0},
        in_specs=[whole()] * 5 + [whole(pltpu.HBM)],
        out_specs=whole(pltpu.HBM),
        scratch_shapes=[
            pltpu.VMEM((3, 8, EXT), F32),
            pltpu.VMEM((3, 8, EXT), F32),
            pltpu.VMEM((2, 8, 1, EXT), F32),
            pltpu.VMEM((2, LEV_DEV, ROWS, EXT), F32),
            pltpu.VMEM((4, *slot), F32),
            pltpu.SemaphoreType.DMA((4,)),
        ],
    )(*map(keep, (south, north, first, last, part)), winds)
    columns = lax.all_to_all(outgoing, "lev", split_axis=0, concat_axis=0, tiled=True)
    total = jnp.sum(sigma_weights)
    sigma = jnp.cumsum(sigma_weights) / total
    inverse = total / sigma_weights
    sigma_row = jnp.pad(sigma, (0, 128 - LEVELS), constant_values=2.0).reshape(1, 128)
    shape = jax.ShapeDtypeStruct((LEVELS, ROWS, PIECE), F32)
    return pl.pallas_call(
        remap_kernel,
        name="remap",
        compiler_params=pltpu.CompilerParams(vmem_limit_bytes=24 << 20),
        out_shape=(shape, shape),
        in_specs=[whole(pltpu.SMEM)] * 2 + [whole()] * 2,
        out_specs=(whole(pltpu.HBM), whole(pltpu.HBM)),
        scratch_shapes=[
            pltpu.VMEM((LEVELS + WINDOW, 2, 9, 8, 128), F32),
            pltpu.VMEM((LEVELS, 2, 8, 128), F32),
            pltpu.VMEM((2, LEVELS, 2, 8, 128), F32),
            pltpu.VMEM((2, LEVELS + LEVELS // 2, 8, 128), F32),
            pltpu.VMEM((2, 64, 128), F32),
            pltpu.VMEM((2, LEVELS // 8, 8, 128), F32),
            pltpu.VMEM((8, 128), jnp.int32),
            pltpu.SMEM((8, 128), jnp.int32),
            pltpu.VMEM((LEVELS, ROWS, PIECE), F32),
            pltpu.VMEM((LEVELS, ROWS, PIECE), F32),
            pltpu.SemaphoreType.DMA((2, LEVELS // BLOCK)),
            pltpu.SemaphoreType.DMA,
        ],
    )(sigma, inverse, sigma_row, keep(columns))


def solution(mesh):
    field = P("lev", "lat", None)
    out = P(None, "lat", "lev")
    return jax.shard_map(
        local,
        mesh=mesh,
        in_specs=(field, field, field, field, P(), P()),
        out_specs=(out, out),
        check_vma=False,
    )
```
